256 devices in a mesh: mem: 32 (over z, y), lat: 8 (over x, core).
Axes of the slice: x: 4, y: 4, z: 8, core: 2. Of those that a mesh axis runs over, the one named last changes fastest.
Arguments:
- background_members: float32 [256, 128, 2048], P('mem', 'lat'), may hold values from -12 to 12
- stencil_weight_table: float32 [5, 128, 2048], P(None, 'lat'), may hold values from 0.034 to 0.637, as said below
- obs_index: int32 [8, 64, 1024], P('lat', 'mem'), may hold values from 0 to 511
- obs_count: int32 [8, 64], P('lat', 'mem'), may hold values from 1 to 1024, as said below
- obs_value: float32 [8, 64, 1024], P('lat', 'mem'), may hold values from -6 to 6
- obs_weight: float32 [8, 64, 1024], P('lat', 'mem'), may hold values from 1 to 16
Outputs:
- analysis: float32 [256, 128, 2048], P('mem', 'lat')
The draws below stay inside these ranges and needn't reach their ends.
Inputs may be any that keep to these rules, and one draw needn't show every extreme that they name: `obs_count`: each patch uses at most 1024 observations, and some patch uses exactly 1024. `stencil_weight_table`: at every cell the five weights sum to 1.
All inputs are finite; a program needn't handle non-finite values.
Results may differ from the reference program's by a relative error of at most 0.0003.
Values sent between devices are 32-bit elements; how exact they have to be, the bound alone decides.
No kernel may reach another device: no remote copies, remote signals or barrier semaphores. Data moves between devices by JAX's collectives and lax.ppermute only.
A program may use at most 64 MiB of HBM per device.

```python
import math
import jax
import jax.numpy as jnp
from jax import lax

MEMBERSHIP_SIZE = 256
LOCAL_AREA_SIZE = 512
NOBS = 1024
NS_ITERS = 8
NLON = 2048
BANDS = 8
BAND_PATCHES = 64
NLAT = 128


def draw_obs_count(key, part):
    first_key, second_key, third_key = jax.random.split(jax.random.fold_in(key, 7), 3)
    shape_here = (BANDS, BAND_PATCHES)
    first_draw = jax.random.randint(first_key, shape_here, 1, NOBS + 1)
    second_draw = jax.random.randint(second_key, shape_here, 1, NOBS + 1)
    counts = jnp.maximum(1, first_draw * second_draw // NOBS)
    position = jax.random.randint(third_key, (), 0, BANDS * BAND_PATCHES)
    flat_counts = jnp.where(jnp.arange(BANDS * BAND_PATCHES) == position, NOBS, counts.reshape(-1))
    return flat_counts.reshape(shape_here).astype(jnp.int32)


def draw_stencil_weight_table(key, part):
    stencil_key = jax.random.fold_in(key, 11)
    shape_here = (5, NLAT, NLON)
    low_log = jnp.log(jnp.float32(0.05))
    high_log = jnp.log(jnp.float32(0.35))
    raw_weights = jnp.exp(jax.random.uniform(stencil_key, shape_here, jnp.float32, low_log, high_log))
    raw_weights = jnp.clip(raw_weights, 0.05, 0.35)
    return (raw_weights / jnp.sum(raw_weights, axis=0, keepdims=True)).astype(jnp.float32)


def set_ends(result, key, smallest, largest):
    shape = result.shape
    spot = [jax.random.randint(jax.random.fold_in(key, axis), (), 0, shape[axis]) for axis in range(len(shape))]
    result = result.at[tuple(spot)].set(smallest)
    longest = shape.index(max(shape))
    spot[longest] = (spot[longest] + 1) % shape[longest]
    return result.at[tuple(spot)].set(largest)


def levels(rng, extent, cuts, smallest, largest):
    level = 1.0
    for dim, blocks in cuts:
        steps = jax.random.uniform(jax.random.fold_in(jax.random.fold_in(rng, 6), dim), (blocks,), jnp.float32, smallest / len(cuts), largest / len(cuts))
        level = level * jnp.repeat(jnp.exp(steps), extent[dim] // blocks).reshape((-1,) + (1,) * (len(extent) - 1 - dim))
    return level


def scatter_about(stream_key, dims, width, limit, pieces=(), kind=jnp.bfloat16):
    array = jax.random.normal(stream_key, dims, jnp.float32) * width
    if len(pieces) > 0:
        array = levels(stream_key, dims, pieces, -0.22, 0.18) * array
    return jnp.clip(array, min=-limit, max=limit).astype(kind)


def setup_inputs(seed: int = 0) -> dict:
    key_list = jax.random.split(jax.random.key(seed), 7)
    return {
        "background_members": scatter_about(key_list[0], (MEMBERSHIP_SIZE, NLAT, NLON), 2.0, 12.0, ((0, 32), (1, 8)), jnp.float32),
        "stencil_weight_table": draw_stencil_weight_table(jax.random.fold_in(key_list[6], 71), 0),
        "obs_index": set_ends(jax.random.randint(key_list[2], (BANDS, BAND_PATCHES, NOBS), 0, LOCAL_AREA_SIZE), jax.random.fold_in(key_list[2], 1), 0, LOCAL_AREA_SIZE - 1).astype(jnp.int32),
        "obs_count": draw_obs_count(jax.random.fold_in(key_list[6], 71), 0),
        "obs_value": scatter_about(key_list[4], (BANDS, BAND_PATCHES, NOBS), 1.0, 6.0, ((0, 8), (1, 32)), jnp.float32),
        "obs_weight": jnp.clip(jnp.exp(math.log(16.0) - 2.7725887 * jax.random.uniform(key_list[5], (BANDS, BAND_PATCHES, NOBS), jnp.float32) ** levels(key_list[5], (BANDS, BAND_PATCHES, NOBS), ((0, 8), (1, 32)), -0.2, 0.2)), 1.0, 16.0),
    }


highest_mode = lax.Precision.HIGHEST

def propagate_once(field, stencil_weight_table):
    north_row = jnp.pad(field[:-1], ((1, 0), (0, 0)))
    south_row = jnp.pad(field[1:], ((0, 1), (0, 0)))
    east_cell = jnp.roll(field, -1, axis=1)
    west_cell = jnp.roll(field, 1, axis=1)
    return stencil_weight_table[0] * field + stencil_weight_table[1] * north_row + stencil_weight_table[2] * south_row + stencil_weight_table[3] * east_cell + stencil_weight_table[4] * west_cell

def analyse(patch_block, indices, obs_total, obs_values, obs_weights):
    identity = jnp.eye(MEMBERSHIP_SIZE, dtype=jnp.float32)
    mean_row = lax.optimization_barrier(jnp.mean(patch_block, axis=0))
    spread = patch_block - mean_row
    weights = jnp.where(jnp.arange(NOBS, dtype=jnp.int32) < obs_total, obs_weights, 0.0)
    observed = jnp.take(spread, indices, axis=1)
    innovation = obs_values - jnp.take(mean_row, indices)
    precision_matrix = jnp.dot(observed * weights, observed.T, precision=highest_mode) + (MEMBERSHIP_SIZE - 1.0) * identity
    projected = jnp.dot(observed, weights * innovation, precision=highest_mode)
    scale = jnp.sqrt(jnp.sum(precision_matrix * precision_matrix))
    approx_root = precision_matrix / scale
    inverse_root = identity
    for repeat in range(NS_ITERS):
        correction = 1.5 * identity - 0.5 * jnp.dot(inverse_root, approx_root, precision=highest_mode)
        approx_root = jnp.dot(approx_root, correction, precision=highest_mode)
        inverse_root = jnp.dot(correction, inverse_root, precision=highest_mode)
    inverse_root = inverse_root / jnp.sqrt(scale)
    mean_weights = jnp.dot(inverse_root, jnp.dot(inverse_root, projected, precision=highest_mode), precision=highest_mode)
    transform = jnp.sqrt(MEMBERSHIP_SIZE - 1.0) * inverse_root + mean_weights[:, None]
    return mean_row + jnp.dot(transform.T, spread, precision=highest_mode)

def reference(background_members, stencil_weight_table, obs_index, obs_count, obs_value, obs_weight):
    advance_prediction = lax.map(lambda single_sample_field: propagate_once(propagate_once(single_sample_field, stencil_weight_table), stencil_weight_table), background_members)
    local_area_number = BANDS * BAND_PATCHES
    mesh_locations = advance_prediction.reshape(MEMBERSHIP_SIZE, local_area_number, LOCAL_AREA_SIZE)
    flat_index = obs_index.reshape(local_area_number, NOBS)
    flat_count = obs_count.reshape(local_area_number)
    flat_value = obs_value.reshape(local_area_number, NOBS)
    flat_weight = obs_weight.reshape(local_area_number, NOBS)

    def one_patch(patch_no):
        patch_block = lax.dynamic_index_in_dim(mesh_locations, patch_no, 1, keepdims=False)
        return analyse(patch_block, flat_index[patch_no], flat_count[patch_no], flat_value[patch_no], flat_weight[patch_no])
    finished = lax.map(one_patch, jnp.arange(local_area_number, dtype=jnp.int32))
    return jnp.transpose(finished, (1, 0, 2)).reshape(MEMBERSHIP_SIZE, NLAT, NLON)
```

```python
import jax
import jax.numpy as jnp
from jax import lax
from jax.experimental import pallas as pl
from jax.experimental.pallas import tpu as pltpu
from jax.sharding import PartitionSpec as P

NS_ITERS = 8
LANES = 128
NN = (((1,), (0,)), ((), ()))
NT = (((1,), (1,)), ((), ()))


def extended(array, sides, width):
    for axis, dim in sides:
        peers, length = (lax.axis_size(axis), array.shape[dim])
        up = [(i, (i + 1) % peers) for i in range(peers - 1)]
        down = [(j, i) for i, j in up]
        last = lax.slice_in_dim(array, length - width, length, axis=dim)
        leading = lax.slice_in_dim(array, 0, width, axis=dim)
        before = lax.ppermute(last, axis, up)
        after = lax.ppermute(leading, axis, down)
        array = jnp.concatenate([before, array, after], axis=dim)
    return array


def propagate_once(border_extended_field, coef_rows):
    centre = border_extended_field[:, 1:-1]
    return (
        coef_rows[0] * centre
        + coef_rows[1] * border_extended_field[:, :-2]
        + coef_rows[2] * border_extended_field[:, 2:]
        + coef_rows[3] * jnp.roll(centre, -1, axis=2)
        + coef_rows[4] * jnp.roll(centre, 1, axis=2)
    )


def halves(x):
    lead = x.astype(jnp.bfloat16)
    return lead, (x - lead.astype(jnp.float32)).astype(jnp.bfloat16)


def dot_of(a, b, dims=NN):
    (ah, al), (bh, bl) = a, b
    dot = lambda p, q: lax.dot_general(p, q, dims, preferred_element_type=jnp.float32)
    return dot(ah, bh) + (dot(ah, bl) + dot(al, bh))


def cell_sums(indices, weights, values, cells):
    groups = cells // LANES
    group, lane = indices // LANES, indices % LANES
    row = lax.broadcasted_iota(jnp.int32, (2 * groups, indices.shape[1]), 0)
    both = jnp.where(row < groups, weights, weights * values)
    left = jnp.where(row % groups == group, both, 0.0)
    hit = lax.broadcasted_iota(jnp.int32, (LANES, indices.shape[1]), 0) == lane
    right = jnp.where(hit, 1.0, 0.0).astype(jnp.bfloat16)
    first = left.astype(jnp.bfloat16)
    rest = left - first.astype(jnp.float32)
    second = rest.astype(jnp.bfloat16)
    third = (rest - second.astype(jnp.float32)).astype(jnp.bfloat16)
    total = 0.0
    for part in (third, second, first):
        total += lax.dot_general(part, right, NT, preferred_element_type=jnp.float32)
    rows = [
        jnp.concatenate([total[s + g : s + g + 1] for g in range(groups)], axis=1)
        for s in (0, groups)
    ]
    return rows


def analysis_kernel(count_ref, index_ref, value_ref, weight_ref, x_ref, out_ref, y_ref, z_ref, s_ref):
    members = x_ref.shape[0]
    patches = index_ref.shape[0]
    cells = x_ref.shape[1] // patches
    identity = jnp.where(
        lax.broadcasted_iota(jnp.int32, (members, members), 0)
        == lax.broadcasted_iota(jnp.int32, (members, members), 1),
        1.0,
        0.0,
    )
    slot = lax.broadcasted_iota(jnp.int32, (1, index_ref.shape[1]), 1)
    scales, means, projections = [], [], []
    for b in range(patches):
        x = x_ref[:, b * cells : (b + 1) * cells]
        mean = jnp.sum(x, axis=0, keepdims=True) * (1.0 / members)
        spread = x - mean
        s_ref[b] = spread
        weights = jnp.where(slot < count_ref[0, b], weight_ref[b : b + 1, :], 0.0)
        weight_sum, value_sum = cell_sums(
            index_ref[b : b + 1, :], weights, value_ref[b : b + 1, :], cells
        )
        misfit = value_sum - weight_sum * mean
        split = halves(spread)
        gram = dot_of(halves(spread * weight_sum), split, NT) + (members - 1.0) * identity
        projected = dot_of(halves(jnp.broadcast_to(misfit, (8, cells))), split, NT)
        scale = jnp.sqrt(jnp.sum(gram * gram, keepdims=True))
        start = gram / scale
        step = halves(start)
        y_ref[b] = 1.5 * start - 0.5 * dot_of(step, step)
        z_ref[b] = 1.5 * identity - 0.5 * start
        scales.append(scale)
        means.append(mean)
        projections.append(projected)

    def iterate(_, carry):
        for b in range(patches):
            y, z = y_ref[b], z_ref[b]
            ys, zs = halves(y), halves(z)
            error = halves(identity - dot_of(zs, ys))
            y_ref[b] = y + 0.5 * dot_of(ys, error)
            z_ref[b] = z + 0.5 * dot_of(error, zs)
        return carry

    lax.fori_loop(0, NS_ITERS - 2, iterate, 0)
    for b in range(patches):
        z = z_ref[b]
        zs = halves(z)
        error = halves(identity - dot_of(zs, halves(y_ref[b])))
        root = halves(z + 0.5 * dot_of(error, zs))
        turned = dot_of(root, halves(s_ref[b]))
        along = dot_of(halves(projections[b]), root)
        shift = dot_of(halves(along), halves(turned))[:1] / scales[b]
        gain = jnp.sqrt((members - 1.0) / scales[b])
        out_ref[:, b * cells : (b + 1) * cells] = (means[b] + shift) + gain * turned


def analyse(arrived, obs_index, obs_count, obs_value, obs_weight):
    members, width = arrived.shape
    patches = obs_index.shape[0]
    vmem = pl.BlockSpec(memory_space=pltpu.VMEM)
    return pl.pallas_call(
        analysis_kernel,
        out_shape=jax.ShapeDtypeStruct(arrived.shape, jnp.float32),
        in_specs=[pl.BlockSpec(memory_space=pltpu.SMEM)] + [vmem] * 4,
        out_specs=vmem,
        scratch_shapes=[
            pltpu.VMEM((patches, members, members), jnp.float32),
            pltpu.VMEM((patches, members, members), jnp.float32),
            pltpu.VMEM((patches, members, width // patches), jnp.float32),
        ],
        name="analysis",
    )(obs_count, obs_index, obs_value, obs_weight, arrived)


def body(background_members, stencil_weight_table, obs_index, obs_count, obs_value, obs_weight):
    member_slice, lat_rows, lon_cells = background_members.shape
    stacked = jnp.concatenate([background_members, stencil_weight_table], axis=0)
    border_extended_field = extended(stacked, (("lat", 1),), 2)
    middle = propagate_once(
        border_extended_field[:member_slice], border_extended_field[member_slice:, 1:-1]
    )
    advance_prediction = propagate_once(middle, stencil_weight_table)
    devices = lax.axis_size("mem")
    width = lat_rows * lon_cells // devices
    outgoing = jnp.swapaxes(advance_prediction.reshape(member_slice, devices, width), 0, 1)
    arrived = lax.all_to_all(outgoing, "mem", split_axis=0, concat_axis=0, tiled=True)
    analysed = analyse(
        arrived.reshape(devices * member_slice, width),
        obs_index[0],
        obs_count,
        obs_value[0],
        obs_weight[0],
    )
    returned = lax.all_to_all(
        analysed.reshape(devices, member_slice, width), "mem", split_axis=0, concat_axis=0, tiled=True
    )
    return jnp.swapaxes(returned, 0, 1).reshape(member_slice, lat_rows, lon_cells)


def solution(mesh):
    placed = (
        P("mem", "lat", None),
        P(None, "lat", None),
        P("lat", "mem", None),
        P("lat", "mem"),
        P("lat", "mem", None),
        P("lat", "mem", None),
    )
    return jax.shard_map(
        body, mesh=mesh, in_specs=placed, out_specs=P("mem", "lat", None), check_vma=False
    )
```

```python
import functools

import jax
import jax.numpy as jnp
from jax import lax
from jax.experimental import pallas as pl
from jax.experimental.pallas import tpu as pltpu
from jax.sharding import PartitionSpec as P

NS_ITERS = 8
LANES = 128
NN = (((1,), (0,)), ((), ()))
NT = (((1,), (1,)), ((), ()))


def edge_kernel(x_hbm, w_hbm, pair_ref, cross_ref, x_ref, w_ref, sems):
    copies = [
        pltpu.make_async_copy(x_hbm, x_ref, sems.at[0]),
        pltpu.make_async_copy(w_hbm, w_ref, sems.at[1]),
    ]
    for copy in copies:
        copy.start()
    for copy in copies:
        copy.wait()
    members, rows, lons = x_ref.shape
    even = lax.rem(lax.axis_index("lat"), 2) == 0

    def pack(out_ref, near, far):
        for k in range(members):
            out_ref[k : k + 1, :lons] = x_ref[k, near : near + 1]
            out_ref[k : k + 1, lons : 2 * lons] = x_ref[k, far : far + 1]
        for run in range(5 * lons // LANES):
            t, start = run // (lons // LANES), run % (lons // LANES) * LANES
            place = 2 * lons + run // members * LANES
            out_ref[run % members : run % members + 1, place : place + LANES] = w_ref[
                t, near : near + 1, start : start + LANES
            ]

    @pl.when(even)
    def _():
        pack(pair_ref, rows - 1, rows - 2)
        pack(cross_ref, 0, 1)

    @pl.when(jnp.logical_not(even))
    def _():
        pack(pair_ref, 0, 1)
        pack(cross_ref, rows - 1, rows - 2)


def step(src_ref, r, weights):
    members, lons = src_ref.shape[1:]
    centre = src_ref[r]
    wide = lambda t: jnp.broadcast_to(weights(t), (members, lons))
    return (
        wide(0) * centre
        + wide(1) * src_ref[r - 1]
        + wide(2) * src_ref[r + 1]
        + wide(3) * pltpu.roll(centre, lons - 1, 1)
        + wide(4) * pltpu.roll(centre, 1, 1)
    )


def inner_kernel(x_ref, w_ref, middle_ref, outer_ref, field_ref):
    rows, members, lons = field_ref.shape
    tiles = lons // LANES

    def gather(r, carry):
        for j in range(tiles):
            start = (r // 8 * tiles + j) * 8 + r % 8
            field_ref[r, :, j * LANES : (j + 1) * LANES] = x_ref[
                pl.ds(start, members, stride=rows * tiles), :
            ]
        return carry

    lax.fori_loop(0, rows, gather, 0)
    for place, r in enumerate((0, 1, rows - 2, rows - 1)):
        outer_ref[place] = field_ref[r]

    def first(r, carry):
        middle_ref[r + 1] = step(field_ref, r, lambda t: w_ref[t, pl.ds(r, 1)])
        return carry

    lax.fori_loop(1, rows - 1, first, 0)


def stencil_kernel(middle_in, outer_ref, w_ref, pair_ref, cross_ref, out_ref, side_ref, rim_ref, near_ref):
    rows_all, members, lons = middle_in.shape
    rows = rows_all - 2
    half = out_ref.shape[2]
    even = lax.rem(lax.axis_index("lat"), 2) == 0

    def unpack(ref, near, far, side):
        rim_ref[near] = ref[:, :lons]
        rim_ref[far] = ref[:, lons : 2 * lons]
        for run in range(5 * lons // LANES):
            t, start = run // (lons // LANES), run % (lons // LANES) * LANES
            place = 2 * lons + run // members * LANES
            side_ref[side, t : t + 1, start : start + LANES] = ref[
                run % members : run % members + 1, place : place + LANES
            ]

    @pl.when(even)
    def _():
        unpack(pair_ref, 6, 7, 1)
        unpack(cross_ref, 1, 0, 0)

    @pl.when(jnp.logical_not(even))
    def _():
        unpack(pair_ref, 1, 0, 0)
        unpack(cross_ref, 6, 7, 1)

    for place in range(4):
        rim_ref[place + 2] = outer_ref[place]
    for side, first, second in ((0, 2, 3), (1, rows - 2, rows - 1)):
        near_ref[side, 2 - 2 * side] = middle_in[first]
        near_ref[side, 3 - 2 * side] = middle_in[second]
    near_ref[0, 0] = step(rim_ref, 1, lambda t: side_ref[0, t : t + 1])
    near_ref[0, 1] = step(rim_ref, 2, lambda t: w_ref[t, 0:1])
    near_ref[1, 2] = step(rim_ref, 5, lambda t: w_ref[t, rows - 1 : rows])
    near_ref[1, 3] = step(rim_ref, 6, lambda t: side_ref[1, t : t + 1])

    def put(r, done):
        for h in range(lons // half):
            out_ref[r * (lons // half) + h] = done[:, h * half : (h + 1) * half]

    def second(r, carry):
        put(r, step(middle_in, r + 1, lambda t: w_ref[t, pl.ds(r, 1)]))
        return carry

    lax.fori_loop(2, rows - 2, second, 0)
    for side, place, r in ((0, 1, 0), (0, 2, 1), (1, 1, rows - 2), (1, 2, rows - 1)):
        put(r, step(near_ref.at[side], place, lambda t: w_ref[t, r : r + 1]))


def return_kernel(in_ref, out_hbm, tile_ref, sems, *, lons):
    members = sems.shape[0]
    size = out_hbm.shape[0] // members
    tiles = lons // LANES
    copies = []
    for member in range(members):
        for block in range(size // (8 * tiles)):
            for j in range(tiles):
                start = (block * 8 * tiles + j) * members + member
                place = member * size + (block * tiles + j) * 8
                tile_ref[place : place + 8, :] = in_ref[pl.ds(start, 8, stride=tiles * members), :]
        part = pl.ds(member * size, size)
        copies.append(pltpu.make_async_copy(tile_ref.at[part], out_hbm.at[part], sems.at[member]))
        copies[-1].start()
    for copy in copies:
        copy.wait()


def sums_kernel(count_ref, index_ref, value_ref, weight_ref, out_ref):
    slot = lax.broadcasted_iota(jnp.int32, (1, index_ref.shape[1]), 1)
    for b in range(index_ref.shape[0]):
        weights = jnp.where(slot < count_ref[0, b], weight_ref[b : b + 1, :], 0.0)
        weight_sum, value_sum = cell_sums(
            index_ref[b : b + 1, :], weights, value_ref[b : b + 1, :], out_ref.shape[2]
        )
        out_ref[b, 0:1] = weight_sum
        out_ref[b, 1:2] = value_sum


def observation_sums(obs_index, obs_count, obs_value, obs_weight, cells):
    vmem = pl.BlockSpec(memory_space=pltpu.VMEM)
    return pl.pallas_call(
        sums_kernel,
        out_shape=jax.ShapeDtypeStruct((obs_index.shape[0], 8, cells), jnp.float32),
        in_specs=[pl.BlockSpec(memory_space=pltpu.SMEM)] + [vmem] * 3,
        out_specs=vmem,
        name="sums",
        compiler_params=pltpu.CompilerParams(vmem_limit_bytes=12 << 20),
        cost_estimate=pl.CostEstimate(flops=10**9, bytes_accessed=10**6, transcendentals=0),
    )(obs_count, obs_index, obs_value, obs_weight)


def by_tile(x):
    a, rows, lanes = x.shape
    x = x.reshape(a, rows // 8, 8, lanes // LANES, LANES)
    return jnp.swapaxes(x, 2, 3).reshape(-1, LANES)


def from_tiles(x, a, rows, lanes):
    x = x.reshape(a, rows // 8, lanes // LANES, 8, LANES)
    return jnp.swapaxes(x, 2, 3).reshape(a, rows, lanes)


def halves(x):
    lead = x.astype(jnp.bfloat16)
    return lead, (x - lead.astype(jnp.float32)).astype(jnp.bfloat16)


def dot_of(a, b, dims=NN):
    (ah, al), (bh, bl) = a, b
    dot = lambda p, q: lax.dot_general(p, q, dims, preferred_element_type=jnp.float32)
    return dot(ah, bh) + (dot(ah, bl) + dot(al, bh))


def cell_sums(indices, weights, values, cells):
    groups = cells // LANES
    group, lane = indices // LANES, indices % LANES
    row = lax.broadcasted_iota(jnp.int32, (2 * groups, indices.shape[1]), 0)
    both = jnp.where(row < groups, weights, weights * values)
    left = jnp.where(row % groups == group, both, 0.0)
    hit = lax.broadcasted_iota(jnp.int32, (LANES, indices.shape[1]), 0) == lane
    right = jnp.where(hit, 1.0, 0.0).astype(jnp.bfloat16)
    first = left.astype(jnp.bfloat16)
    rest = left - first.astype(jnp.float32)
    second = rest.astype(jnp.bfloat16)
    third = (rest - second.astype(jnp.float32)).astype(jnp.bfloat16)
    total = 0.0
    for part in (third, second, first):
        total += lax.dot_general(part, right, NT, preferred_element_type=jnp.float32)
    rows = [
        jnp.concatenate([total[s + g : s + g + 1] for g in range(groups)], axis=1)
        for s in (0, groups)
    ]
    return rows


def analysis_kernel(sums_ref, x_ref, out_ref, y_ref, z_ref, s_ref):
    members = x_ref.shape[0]
    patches = sums_ref.shape[0]
    cells = x_ref.shape[1] // patches
    identity = jnp.where(
        lax.broadcasted_iota(jnp.int32, (members, members), 0)
        == lax.broadcasted_iota(jnp.int32, (members, members), 1),
        1.0,
        0.0,
    )
    scales, means, projections = [], [], []
    for b in range(patches):
        x = x_ref[:, b * cells : (b + 1) * cells]
        mean = jnp.sum(x, axis=0, keepdims=True) * (1.0 / members)
        spread = x - mean
        s_ref[b] = spread
        weight_sum, value_sum = sums_ref[b, 0:1], sums_ref[b, 1:2]
        misfit = value_sum - weight_sum * mean
        split = halves(spread)
        gram = dot_of(halves(spread * weight_sum), split, NT) + (members - 1.0) * identity
        projected = dot_of(halves(jnp.broadcast_to(misfit, (8, cells))), split, NT)
        scale = jnp.sqrt(jnp.sum(gram * gram, keepdims=True))
        start = gram / scale
        step = halves(start)
        y_ref[b] = 1.5 * start - 0.5 * dot_of(step, step)
        z_ref[b] = 1.5 * identity - 0.5 * start
        scales.append(scale)
        means.append(mean)
        projections.append(projected)

    def iterate(_, carry):
        for b in range(patches):
            y, z = y_ref[b], z_ref[b]
            ys, zs = halves(y), halves(z)
            error = halves(identity - dot_of(zs, ys))
            y_ref[b] = y + 0.5 * dot_of(ys, error)
            z_ref[b] = z + 0.5 * dot_of(error, zs)
        return carry

    lax.fori_loop(0, NS_ITERS - 2, iterate, 0)
    for b in range(patches):
        z = z_ref[b]
        zs = halves(z)
        error = halves(identity - dot_of(zs, halves(y_ref[b])))
        root = halves(z + 0.5 * dot_of(error, zs))
        turned = dot_of(root, halves(s_ref[b]))
        along = dot_of(halves(projections[b]), root)
        shift = dot_of(halves(along), halves(turned))[:1] / scales[b]
        gain = jnp.sqrt((members - 1.0) / scales[b])
        out_ref[:, b * cells : (b + 1) * cells] = (means[b] + shift) + gain * turned


def analyse(arrived, sums):
    members, width = arrived.shape
    patches = sums.shape[0]
    vmem = pl.BlockSpec(memory_space=pltpu.VMEM)
    return pl.pallas_call(
        analysis_kernel,
        out_shape=jax.ShapeDtypeStruct(arrived.shape, jnp.float32),
        in_specs=[vmem] * 2,
        out_specs=vmem,
        scratch_shapes=[
            pltpu.VMEM((patches, members, members), jnp.float32),
            pltpu.VMEM((patches, members, members), jnp.float32),
            pltpu.VMEM((patches, members, width // patches), jnp.float32),
        ],
        name="analysis",
        compiler_params=pltpu.CompilerParams(vmem_limit_bytes=16 << 20),
    )(sums, arrived)


def forecast(background_members, stencil_weight_table, devices, beside):
    members, rows, lons = background_members.shape
    width = rows * lons // devices
    vmem = pl.BlockSpec(memory_space=pltpu.VMEM)
    hbm = pl.BlockSpec(memory_space=pltpu.HBM)
    small = pltpu.CompilerParams(vmem_limit_bytes=12 << 20)
    packed = jax.ShapeDtypeStruct((members, 2 * lons + 5 * lons // members), jnp.float32)
    pair, cross = pl.pallas_call(
        edge_kernel,
        out_shape=[packed, packed],
        in_specs=[hbm] * 2,
        out_specs=[vmem] * 2,
        scratch_shapes=[
            pltpu.VMEM(background_members.shape, jnp.float32),
            pltpu.VMEM(stencil_weight_table.shape, jnp.float32),
            pltpu.SemaphoreType.DMA((2,)),
        ],
        name="edges",
        compiler_params=small,
    )(
        pltpu.with_memory_space_constraint(background_members, pltpu.HBM),
        pltpu.with_memory_space_constraint(stencil_weight_table, pltpu.HBM),
    )
    bands = lax.axis_size("lat")
    within = [(i, i ^ 1) for i in range(bands)]
    across = [(i, i - 1 + 2 * (i % 2)) for i in range(1, bands - 1)]
    cross = lax.ppermute(cross, "lat", across)
    pair = lax.ppermute(pair, "lat", within)
    middle, outer = pl.pallas_call(
        inner_kernel,
        out_shape=[
            jax.ShapeDtypeStruct((rows + 2, members, lons), jnp.float32),
            jax.ShapeDtypeStruct((4, members, lons), jnp.float32),
        ],
        in_specs=[vmem] * 2,
        out_specs=[vmem] * 2,
        scratch_shapes=[pltpu.VMEM((rows, members, lons), jnp.float32)],
        name="inner",
        compiler_params=small,
        cost_estimate=pl.CostEstimate(flops=10**9, bytes_accessed=4 * 10**6, transcendentals=0),
    )(by_tile(background_members), stencil_weight_table)
    middle, beside = lax.optimization_barrier((middle, beside))
    pieces = pl.pallas_call(
        stencil_kernel,
        out_shape=jax.ShapeDtypeStruct((devices, members, width), jnp.float32),
        in_specs=[vmem] * 5,
        out_specs=vmem,
        scratch_shapes=[
            pltpu.VMEM((2, 8, lons), jnp.float32),
            pltpu.VMEM((8, members, lons), jnp.float32),
            pltpu.VMEM((2, 4, members, lons), jnp.float32),
        ],
        name="stencil",
        compiler_params=small,
    )(middle, outer, stencil_weight_table, pair, cross)
    return pieces, beside


def body(background_members, stencil_weight_table, obs_index, obs_count, obs_value, obs_weight):
    member_slice, lat_rows, lon_cells = background_members.shape
    devices = lax.axis_size("mem")
    width = lat_rows * lon_cells // devices
    patches = obs_index.shape[1]
    sums = observation_sums(obs_index[0], obs_count, obs_value[0], obs_weight[0], width // patches)
    outgoing, sums = forecast(background_members, stencil_weight_table, devices, sums)
    arrived = lax.all_to_all(outgoing, "mem", split_axis=0, concat_axis=0, tiled=True)
    analysed = analyse(arrived.reshape(devices * member_slice, width), sums)
    returned = lax.all_to_all(
        analysed.reshape(devices, member_slice, width), "mem", split_axis=0, concat_axis=0, tiled=True
    )
    result = pl.pallas_call(
        functools.partial(return_kernel, lons=lon_cells),
        out_shape=jax.ShapeDtypeStruct((background_members.size // LANES, LANES), jnp.float32),
        in_specs=[pl.BlockSpec(memory_space=pltpu.VMEM)],
        out_specs=pl.BlockSpec(memory_space=pltpu.HBM),
        scratch_shapes=[
            pltpu.VMEM((background_members.size // LANES, LANES), jnp.float32),
            pltpu.SemaphoreType.DMA((member_slice,)),
        ],
        name="home",
        compiler_params=pltpu.CompilerParams(vmem_limit_bytes=12 << 20),
    )(by_tile(returned))
    return from_tiles(result, member_slice, lat_rows, lon_cells)


def solution(mesh):
    placed = (
        P("mem", "lat", None),
        P(None, "lat", None),
        P("lat", "mem", None),
        P("lat", "mem"),
        P("lat", "mem", None),
        P("lat", "mem", None),
    )
    return jax.shard_map(
        body, mesh=mesh, in_specs=placed, out_specs=P("mem", "lat", None), check_vma=False
    )
```

```python
import functools

import jax
import jax.numpy as jnp
from jax import lax
from jax.experimental import pallas as pl
from jax.experimental.pallas import tpu as pltpu
from jax.sharding import PartitionSpec as P

NS_ITERS = 8
LANES = 128
NN = (((1,), (0,)), ((), ()))
NT = (((1,), (1,)), ((), ()))


def edge_kernel(x_hbm, w_hbm, pair_ref, cross_ref, x_ref, w_ref, sems):
    copies = [
        pltpu.make_async_copy(x_hbm, x_ref, sems.at[0]),
        pltpu.make_async_copy(w_hbm, w_ref, sems.at[1]),
    ]
    for copy in copies:
        copy.start()
    for copy in copies:
        copy.wait()
    members, rows, lons = x_ref.shape
    even = lax.rem(lax.axis_index("lat"), 2) == 0

    def pack(out_ref, near, far):
        for k in range(members):
            out_ref[k : k + 1, :lons] = x_ref[k, near : near + 1]
            out_ref[k : k + 1, lons : 2 * lons] = x_ref[k, far : far + 1]
        for run in range(5 * lons // LANES):
            t, start = run // (lons // LANES), run % (lons // LANES) * LANES
            place = 2 * lons + run // members * LANES
            out_ref[run % members : run % members + 1, place : place + LANES] = w_ref[
                t, near : near + 1, start : start + LANES
            ]

    @pl.when(even)
    def _():
        pack(pair_ref, rows - 1, rows - 2)
        pack(cross_ref, 0, 1)

    @pl.when(jnp.logical_not(even))
    def _():
        pack(pair_ref, 0, 1)
        pack(cross_ref, rows - 1, rows - 2)


def step(src_ref, r, weights):
    members, lons = src_ref.shape[1:]
    centre = src_ref[r]
    wide = lambda t: jnp.broadcast_to(weights(t), (members, lons))
    return (
        wide(0) * centre
        + wide(1) * src_ref[r - 1]
        + wide(2) * src_ref[r + 1]
        + wide(3) * pltpu.roll(centre, lons - 1, 1)
        + wide(4) * pltpu.roll(centre, 1, 1)
    )


def inner_kernel(x_ref, w_ref, middle_ref, outer_ref, field_ref):
    rows, members, lons = field_ref.shape
    tiles = lons // LANES

    def gather(r, carry):
        for j in range(tiles):
            start = (r // 8 * tiles + j) * 8 + r % 8
            field_ref[r, :, j * LANES : (j + 1) * LANES] = x_ref[
                pl.ds(start, members, stride=rows * tiles), :
            ]
        return carry

    lax.fori_loop(0, rows, gather, 0)
    for place, r in enumerate((0, 1, rows - 2, rows - 1)):
        outer_ref[place] = field_ref[r]

    def first(r, carry):
        middle_ref[r + 1] = step(field_ref, r, lambda t: w_ref[t, pl.ds(r, 1)])
        return carry

    lax.fori_loop(1, rows - 1, first, 0)


def stencil_kernel(middle_in, outer_ref, w_ref, pair_ref, cross_ref, out_ref, side_ref, rim_ref, near_ref):
    rows_all, members, lons = middle_in.shape
    rows = rows_all - 2
    half = out_ref.shape[2]
    even = lax.rem(lax.axis_index("lat"), 2) == 0

    def unpack(ref, near, far, side):
        rim_ref[near] = ref[:, :lons]
        rim_ref[far] = ref[:, lons : 2 * lons]
        for run in range(5 * lons // LANES):
            t, start = run // (lons // LANES), run % (lons // LANES) * LANES
            place = 2 * lons + run // members * LANES
            side_ref[side, t : t + 1, start : start + LANES] = ref[
                run % members : run % members + 1, place : place + LANES
            ]

    @pl.when(even)
    def _():
        unpack(pair_ref, 6, 7, 1)
        unpack(cross_ref, 1, 0, 0)

    @pl.when(jnp.logical_not(even))
    def _():
        unpack(pair_ref, 1, 0, 0)
        unpack(cross_ref, 6, 7, 1)

    for place in range(4):
        rim_ref[place + 2] = outer_ref[place]
    for side, first, second in ((0, 2, 3), (1, rows - 2, rows - 1)):
        near_ref[side, 2 - 2 * side] = middle_in[first]
        near_ref[side, 3 - 2 * side] = middle_in[second]
    near_ref[0, 0] = step(rim_ref, 1, lambda t: side_ref[0, t : t + 1])
    near_ref[0, 1] = step(rim_ref, 2, lambda t: w_ref[t, 0:1])
    near_ref[1, 2] = step(rim_ref, 5, lambda t: w_ref[t, rows - 1 : rows])
    near_ref[1, 3] = step(rim_ref, 6, lambda t: side_ref[1, t : t + 1])

    def put(r, done):
        for h in range(lons // half):
            out_ref[r * (lons // half) + h] = done[:, h * half : (h + 1) * half]

    def second(r, carry):
        put(r, step(middle_in, r + 1, lambda t: w_ref[t, pl.ds(r, 1)]))
        return carry

    lax.fori_loop(2, rows - 2, second, 0)
    for side, place, r in ((0, 1, 0), (0, 2, 1), (1, 1, rows - 2), (1, 2, rows - 1)):
        put(r, step(near_ref.at[side], place, lambda t: w_ref[t, r : r + 1]))


def return_kernel(in_ref, out_hbm, tile_ref, sems, *, lons):
    members = sems.shape[0]
    size = out_hbm.shape[0] // members
    tiles = lons // LANES
    copies = []
    for member in range(members):
        for block in range(size // (8 * tiles)):
            for j in range(tiles):
                start = (block * 8 * tiles + j) * members + member
                place = member * size + (block * tiles + j) * 8
                tile_ref[place : place + 8, :] = in_ref[pl.ds(start, 8, stride=tiles * members), :]
        part = pl.ds(member * size, size)
        copies.append(pltpu.make_async_copy(tile_ref.at[part], out_hbm.at[part], sems.at[member]))
        copies[-1].start()
    for copy in copies:
        copy.wait()


def sums_kernel(count_ref, index_ref, value_ref, weight_ref, out_ref):
    slot = lax.broadcasted_iota(jnp.int32, (1, index_ref.shape[1]), 1)
    for b in range(index_ref.shape[0]):
        weights = jnp.where(slot < count_ref[0, b], weight_ref[b : b + 1, :], 0.0)
        weight_sum, value_sum = cell_sums(
            index_ref[b : b + 1, :], weights, value_ref[b : b + 1, :], out_ref.shape[2]
        )
        out_ref[b, 0:1] = weight_sum
        out_ref[b, 1:2] = value_sum


def observation_sums(obs_index, obs_count, obs_value, obs_weight, cells):
    vmem = pl.BlockSpec(memory_space=pltpu.VMEM)
    return pl.pallas_call(
        sums_kernel,
        out_shape=jax.ShapeDtypeStruct((obs_index.shape[0], 8, cells), jnp.float32),
        in_specs=[pl.BlockSpec(memory_space=pltpu.SMEM)] + [vmem] * 3,
        out_specs=vmem,
        name="sums",
        compiler_params=pltpu.CompilerParams(vmem_limit_bytes=12 << 20),
        cost_estimate=pl.CostEstimate(flops=10**9, bytes_accessed=10**6, transcendentals=0),
    )(obs_count, obs_index, obs_value, obs_weight)


def by_tile(x):
    a, rows, lanes = x.shape
    x = x.reshape(a, rows // 8, 8, lanes // LANES, LANES)
    return jnp.swapaxes(x, 2, 3).reshape(-1, LANES)


def from_tiles(x, a, rows, lanes):
    x = x.reshape(a, rows // 8, lanes // LANES, 8, LANES)
    return jnp.swapaxes(x, 2, 3).reshape(a, rows, lanes)


def halves(x):
    lead = x.astype(jnp.bfloat16)
    return lead, (x - lead.astype(jnp.float32)).astype(jnp.bfloat16)


def dot_of(a, b, dims=NN):
    (ah, al), (bh, bl) = a, b
    dot = lambda p, q: lax.dot_general(p, q, dims, preferred_element_type=jnp.float32)
    return dot(ah, bh) + (dot(ah, bl) + dot(al, bh))


def cell_sums(indices, weights, values, cells):
    groups = cells // LANES
    group, lane = indices // LANES, indices % LANES
    row = lax.broadcasted_iota(jnp.int32, (2 * groups, indices.shape[1]), 0)
    both = jnp.where(row < groups, weights, weights * values)
    left = jnp.where(row % groups == group, both, 0.0)
    hit = lax.broadcasted_iota(jnp.int32, (LANES, indices.shape[1]), 0) == lane
    right = jnp.where(hit, 1.0, 0.0).astype(jnp.bfloat16)
    first = left.astype(jnp.bfloat16)
    rest = left - first.astype(jnp.float32)
    second = rest.astype(jnp.bfloat16)
    third = (rest - second.astype(jnp.float32)).astype(jnp.bfloat16)
    total = 0.0
    for part in (third, second, first):
        total += lax.dot_general(part, right, NT, preferred_element_type=jnp.float32)
    rows = [
        jnp.concatenate([total[s + g : s + g + 1] for g in range(groups)], axis=1)
        for s in (0, groups)
    ]
    return rows


def analysis_kernel(sums_ref, x_ref, out_ref, *scratch):
    patches = sums_ref.shape[0]
    members = x_ref.shape[0]
    cells = x_ref.shape[1] // patches
    matrix_ref, root_ref, spread_ref, left_ref, right_ref = scratch[:5]
    totals = [scratch[5 + 3 * b : 8 + 3 * b] for b in range(patches)]
    identity = jnp.where(
        lax.broadcasted_iota(jnp.int32, (members, members), 0)
        == lax.broadcasted_iota(jnp.int32, (members, members), 1),
        1.0,
        0.0,
    )
    each = range(patches)
    chunks = [pl.ds(c, members) for c in range(0, cells, members)]
    LEAD, REST = 0, 1

    def load(b, lead, rest, transpose=False):
        if lead is not None:
            pltpu.matmul_push_rhs(lead, LEAD, b, transpose=transpose)
        if rest is not None:
            pltpu.matmul_push_rhs(rest, REST, b, transpose=transpose)

    stream = lambda total, rows, use=None: pltpu.matmul_acc_lhs(total, rows, load_staged_rhs=use)

    means, projections, scales = [], [], []
    for b in each:
        x = x_ref[:, b * cells : (b + 1) * cells]
        mean = jnp.sum(x, axis=0, keepdims=True) * (1.0 / members)
        spread = x - mean
        weight_sum, value_sum = sums_ref[b, 0:1], sums_ref[b, 1:2]
        spread_ref[b, LEAD], spread_ref[b, REST] = halves(spread)
        left_ref[b, LEAD], left_ref[b, REST] = halves(spread * weight_sum)
        misfit = value_sum - weight_sum * mean
        projections.append(jnp.sum(spread * misfit, axis=1, keepdims=True))
        means.append(mean)
    for chunk in chunks:
        for b in each:
            load(b, spread_ref[b, LEAD, :, chunk], spread_ref[b, REST, :, chunk], transpose=True)
            stream(totals[b][0], left_ref[b, LEAD, :, chunk], LEAD)
            stream(totals[b][0], left_ref[b, REST, :, chunk])
            stream(totals[b][0], left_ref[b, LEAD, :, chunk], REST)
    for b in each:
        gram = pltpu.matmul_pop(totals[b][0]) + (members - 1.0) * identity
        scale = jnp.sqrt(jnp.sum(gram * gram, keepdims=True))
        scales.append(scale)
        start = gram * (1.0 / scale)
        matrix_ref[b] = start
        root_ref[b] = 1.5 * identity - 0.5 * start
        right_ref[b, LEAD], right_ref[b, REST] = halves(start)

    def iterate(with_root):
        for b in each:
            load(b, right_ref[b, LEAD], right_ref[b, REST])
            stream(totals[b][0], right_ref[b, LEAD], LEAD)
            stream(totals[b][0], right_ref[b, REST])
            stream(totals[b][0], right_ref[b, LEAD], REST)
        squares = []
        for b in each:
            if with_root:
                root = halves(root_ref[b])
                left_ref[b, LEAD, :, :members], left_ref[b, REST, :, :members] = root
                stream(totals[b][2], left_ref[b, LEAD, :, :members])
            square = pltpu.matmul_pop(totals[b][0])
            lead, rest = halves(square)
            load(b, right_ref[b, LEAD], None)
            stream(totals[b][1], lead)
            stream(totals[b][1], lead, LEAD)
            stream(totals[b][1], rest)
            squares.append(square)
            if with_root:
                stream(totals[b][2], left_ref[b, LEAD, :, :members])
                stream(totals[b][2], left_ref[b, REST, :, :members])
        for b in each:
            cube = pltpu.matmul_pop(totals[b][1])
            matrix = 2.25 * matrix_ref[b] - 1.5 * squares[b] + 0.25 * cube
            matrix_ref[b] = matrix
            right_ref[b, LEAD], right_ref[b, REST] = halves(matrix)
        if with_root:
            for b in each:
                root_ref[b] = 1.5 * root_ref[b] - 0.5 * pltpu.matmul_pop(totals[b][2])

    iterate(False)

    def body(_, carry):
        iterate(True)
        return carry

    lax.fori_loop(0, NS_ITERS - 2, body, 0)
    roots = []
    for b in each:
        lead, rest = halves(root_ref[b])
        load(b, right_ref[b, LEAD], right_ref[b, REST])
        stream(totals[b][0], lead, LEAD)
        stream(totals[b][0], rest)
        stream(totals[b][0], lead, REST)
    for b in each:
        root = 1.5 * root_ref[b] - 0.5 * pltpu.matmul_pop(totals[b][0])
        root_ref[b] = root
        roots.append(halves(root))
    for c, chunk in enumerate(chunks):
        for b in each:
            load(b, spread_ref[b, LEAD, :, chunk], spread_ref[b, REST, :, chunk])
            stream(totals[b][c], roots[b][0], LEAD)
            stream(totals[b][c], roots[b][1])
            stream(totals[b][c], roots[b][0], REST)
    for b in each:
        along = jnp.sum(root_ref[b] * projections[b], axis=0, keepdims=True)
        mover = jnp.sum(root_ref[b] * along, axis=1, keepdims=True) / scales[b]
        gain = jnp.sqrt((members - 1.0) / scales[b])
        for c, chunk in enumerate(chunks):
            place = slice(b * cells + c * members, b * cells + (c + 1) * members)
            mean = means[b][:, c * members : (c + 1) * members]
            spread = x_ref[:, place] - mean
            shift = mean + jnp.sum(spread * mover, axis=0, keepdims=True)
            out_ref[:, place] = shift + gain * pltpu.matmul_pop(totals[b][c])


def analyse(arrived, sums):
    members, width = arrived.shape
    patches = sums.shape[0]
    cells = width // patches
    vmem = pl.BlockSpec(memory_space=pltpu.VMEM)
    square = (members, members)
    kernel = lambda *refs: pl.run_scoped(
        functools.partial(analysis_kernel, *refs),
        *(pltpu.ACC(b)(square, jnp.float32) for b in range(patches) for _ in range(3)),
    )
    return pl.pallas_call(
        kernel,
        out_shape=jax.ShapeDtypeStruct(arrived.shape, jnp.float32),
        in_specs=[vmem] * 2,
        out_specs=vmem,
        scratch_shapes=[
            pltpu.VMEM((patches, *square), jnp.float32),
            pltpu.VMEM((patches, *square), jnp.float32),
            pltpu.VMEM((patches, 2, members, cells), jnp.bfloat16),
            pltpu.VMEM((patches, 2, members, cells), jnp.bfloat16),
            pltpu.VMEM((patches, 2, *square), jnp.bfloat16),
        ],
        name="analysis",
        compiler_params=pltpu.CompilerParams(vmem_limit_bytes=16 << 20),
    )(sums, arrived)


def forecast(background_members, stencil_weight_table, devices, beside):
    members, rows, lons = background_members.shape
    width = rows * lons // devices
    vmem = pl.BlockSpec(memory_space=pltpu.VMEM)
    hbm = pl.BlockSpec(memory_space=pltpu.HBM)
    small = pltpu.CompilerParams(vmem_limit_bytes=12 << 20)
    packed = jax.ShapeDtypeStruct((members, 2 * lons + 5 * lons // members), jnp.float32)
    pair, cross = pl.pallas_call(
        edge_kernel,
        out_shape=[packed, packed],
        in_specs=[hbm] * 2,
        out_specs=[vmem] * 2,
        scratch_shapes=[
            pltpu.VMEM(background_members.shape, jnp.float32),
            pltpu.VMEM(stencil_weight_table.shape, jnp.float32),
            pltpu.SemaphoreType.DMA((2,)),
        ],
        name="edges",
        compiler_params=small,
    )(
        pltpu.with_memory_space_constraint(background_members, pltpu.HBM),
        pltpu.with_memory_space_constraint(stencil_weight_table, pltpu.HBM),
    )
    bands = lax.axis_size("lat")
    within = [(i, i ^ 1) for i in range(bands)]
    across = [(i, i - 1 + 2 * (i % 2)) for i in range(1, bands - 1)]
    cross = lax.ppermute(cross, "lat", across)
    pair = lax.ppermute(pair, "lat", within)
    middle, outer = pl.pallas_call(
        inner_kernel,
        out_shape=[
            jax.ShapeDtypeStruct((rows + 2, members, lons), jnp.float32),
            jax.ShapeDtypeStruct((4, members, lons), jnp.float32),
        ],
        in_specs=[vmem] * 2,
        out_specs=[vmem] * 2,
        scratch_shapes=[pltpu.VMEM((rows, members, lons), jnp.float32)],
        name="inner",
        compiler_params=small,
        cost_estimate=pl.CostEstimate(flops=10**9, bytes_accessed=4 * 10**6, transcendentals=0),
    )(by_tile(background_members), stencil_weight_table)
    middle, beside = lax.optimization_barrier((middle, beside))
    pieces = pl.pallas_call(
        stencil_kernel,
        out_shape=jax.ShapeDtypeStruct((devices, members, width), jnp.float32),
        in_specs=[vmem] * 5,
        out_specs=vmem,
        scratch_shapes=[
            pltpu.VMEM((2, 8, lons), jnp.float32),
            pltpu.VMEM((8, members, lons), jnp.float32),
            pltpu.VMEM((2, 4, members, lons), jnp.float32),
        ],
        name="stencil",
        compiler_params=small,
    )(middle, outer, stencil_weight_table, pair, cross)
    return pieces, beside


def body(background_members, stencil_weight_table, obs_index, obs_count, obs_value, obs_weight):
    member_slice, lat_rows, lon_cells = background_members.shape
    devices = lax.axis_size("mem")
    width = lat_rows * lon_cells // devices
    patches = obs_index.shape[1]
    sums = observation_sums(obs_index[0], obs_count, obs_value[0], obs_weight[0], width // patches)
    outgoing, sums = forecast(background_members, stencil_weight_table, devices, sums)
    arrived = lax.all_to_all(outgoing, "mem", split_axis=0, concat_axis=0, tiled=True)
    analysed = analyse(arrived.reshape(devices * member_slice, width), sums)
    returned = lax.all_to_all(
        analysed.reshape(devices, member_slice, width), "mem", split_axis=0, concat_axis=0, tiled=True
    )
    result = pl.pallas_call(
        functools.partial(return_kernel, lons=lon_cells),
        out_shape=jax.ShapeDtypeStruct((background_members.size // LANES, LANES), jnp.float32),
        in_specs=[pl.BlockSpec(memory_space=pltpu.VMEM)],
        out_specs=pl.BlockSpec(memory_space=pltpu.HBM),
        scratch_shapes=[
            pltpu.VMEM((background_members.size // LANES, LANES), jnp.float32),
            pltpu.SemaphoreType.DMA((member_slice,)),
        ],
        name="home",
        compiler_params=pltpu.CompilerParams(vmem_limit_bytes=12 << 20),
    )(by_tile(returned))
    return from_tiles(result, member_slice, lat_rows, lon_cells)


def solution(mesh):
    placed = (
        P("mem", "lat", None),
        P(None, "lat", None),
        P("lat", "mem", None),
        P("lat", "mem"),
        P("lat", "mem", None),
        P("lat", "mem", None),
    )
    return jax.shard_map(
        body, mesh=mesh, in_specs=placed, out_specs=P("mem", "lat", None), check_vma=False
    )
```

```python
import functools

import jax
import jax.numpy as jnp
from jax import lax
from jax.experimental import pallas as pl
from jax.experimental.pallas import tpu as pltpu
from jax.sharding import PartitionSpec as P


NS_ITERS = 8
LANES = 128
NT = (((1,), (1,)), ((), ()))


def edge_kernel(x_hbm, w_hbm, pair_ref, cross_ref, x_ref, w_ref, sems):
    copies = [
        pltpu.make_async_copy(x_hbm, x_ref, sems.at[0]),
        pltpu.make_async_copy(w_hbm, w_ref, sems.at[1]),
    ]
    for copy in copies:
        copy.start()
    for copy in copies:
        copy.wait()
    members, rows, lons = x_ref.shape
    even = lax.rem(lax.axis_index("lat"), 2) == 0

    def pack(out_ref, near, far):
        for k in range(members):
            out_ref[k : k + 1, :lons] = x_ref[k, near : near + 1]
            out_ref[k : k + 1, lons : 2 * lons] = x_ref[k, far : far + 1]
        for run in range(5 * lons // LANES):
            t, start = run // (lons // LANES), run % (lons // LANES) * LANES
            place = 2 * lons + run // members * LANES
            out_ref[run % members : run % members + 1, place : place + LANES] = w_ref[
                t, near : near + 1, start : start + LANES
            ]

    @pl.when(even)
    def _():
        pack(pair_ref, rows - 1, rows - 2)
        pack(cross_ref, 0, 1)

    @pl.when(jnp.logical_not(even))
    def _():
        pack(pair_ref, 0, 1)
        pack(cross_ref, rows - 1, rows - 2)


def step(src_ref, r, weights):
    members, lons = src_ref.shape[1:]
    centre = src_ref[r]
    wide = lambda t: jnp.broadcast_to(weights(t), (members, lons))
    return (
        wide(0) * centre
        + wide(1) * src_ref[r - 1]
        + wide(2) * src_ref[r + 1]
        + wide(3) * pltpu.roll(centre, lons - 1, 1)
        + wide(4) * pltpu.roll(centre, 1, 1)
    )


def inner_kernel(x_ref, w_ref, middle_ref, outer_ref, field_ref):
    rows, members, lons = field_ref.shape
    tiles = lons // LANES

    def gather(r, carry):
        for j in range(tiles):
            start = (r // 8 * tiles + j) * 8 + r % 8
            field_ref[r, :, j * LANES : (j + 1) * LANES] = x_ref[
                pl.ds(start, members, stride=rows * tiles), :
            ]
        return carry

    lax.fori_loop(0, rows, gather, 0)
    for place, r in enumerate((0, 1, rows - 2, rows - 1)):
        outer_ref[place] = field_ref[r]

    def first(r, carry):
        middle_ref[r + 1] = step(field_ref, r, lambda t: w_ref[t, pl.ds(r, 1)])
        return carry

    lax.fori_loop(1, rows - 1, first, 0)


def stencil_kernel(middle_in, outer_ref, w_ref, pair_ref, cross_ref, out_ref, side_ref, rim_ref, near_ref):
    rows_all, members, lons = middle_in.shape
    rows = rows_all - 2
    half = out_ref.shape[2]
    even = lax.rem(lax.axis_index("lat"), 2) == 0

    def unpack(ref, near, far, side):
        rim_ref[near] = ref[:, :lons]
        rim_ref[far] = ref[:, lons : 2 * lons]
        for run in range(5 * lons // LANES):
            t, start = run // (lons // LANES), run % (lons // LANES) * LANES
            place = 2 * lons + run // members * LANES
            side_ref[side, t : t + 1, start : start + LANES] = ref[
                run % members : run % members + 1, place : place + LANES
            ]

    @pl.when(even)
    def _():
        unpack(pair_ref, 6, 7, 1)
        unpack(cross_ref, 1, 0, 0)

    @pl.when(jnp.logical_not(even))
    def _():
        unpack(pair_ref, 1, 0, 0)
        unpack(cross_ref, 6, 7, 1)

    for place in range(4):
        rim_ref[place + 2] = outer_ref[place]
    for side, first, second in ((0, 2, 3), (1, rows - 2, rows - 1)):
        near_ref[side, 2 - 2 * side] = middle_in[first]
        near_ref[side, 3 - 2 * side] = middle_in[second]
    near_ref[0, 0] = step(rim_ref, 1, lambda t: side_ref[0, t : t + 1])
    near_ref[0, 1] = step(rim_ref, 2, lambda t: w_ref[t, 0:1])
    near_ref[1, 2] = step(rim_ref, 5, lambda t: w_ref[t, rows - 1 : rows])
    near_ref[1, 3] = step(rim_ref, 6, lambda t: side_ref[1, t : t + 1])

    def put(r, done):
        for h in range(lons // half):
            out_ref[r * (lons // half) + h] = done[:, h * half : (h + 1) * half]

    def second(r, carry):
        put(r, step(middle_in, r + 1, lambda t: w_ref[t, pl.ds(r, 1)]))
        return carry

    lax.fori_loop(2, rows - 2, second, 0)
    for side, place, r in ((0, 1, 0), (0, 2, 1), (1, 1, rows - 2), (1, 2, rows - 1)):
        put(r, step(near_ref.at[side], place, lambda t: w_ref[t, r : r + 1]))


def return_kernel(in_ref, out_hbm, tile_ref, sems, *, lons):
    members = sems.shape[0]
    size = out_hbm.shape[0] // members
    tiles = lons // LANES
    copies = []
    for member in range(members):
        for block in range(size // (8 * tiles)):
            for j in range(tiles):
                start = (block * 8 * tiles + j) * members + member
                place = member * size + (block * tiles + j) * 8
                tile_ref[place : place + 8, :] = in_ref[pl.ds(start, 8, stride=tiles * members), :]
        part = pl.ds(member * size, size)
        copies.append(pltpu.make_async_copy(tile_ref.at[part], out_hbm.at[part], sems.at[member]))
        copies[-1].start()
    for copy in copies:
        copy.wait()


def sums_kernel(count_ref, index_ref, value_ref, weight_ref, out_ref):
    slot = lax.broadcasted_iota(jnp.int32, (1, index_ref.shape[1]), 1)
    for b in range(index_ref.shape[0]):
        weights = jnp.where(slot < count_ref[0, b], weight_ref[b : b + 1, :], 0.0)
        weight_sum, value_sum = cell_sums(
            index_ref[b : b + 1, :], weights, value_ref[b : b + 1, :], out_ref.shape[2]
        )
        out_ref[b, 0:1] = weight_sum
        out_ref[b, 1:2] = value_sum


def observation_sums(obs_index, obs_count, obs_value, obs_weight, cells):
    vmem = pl.BlockSpec(memory_space=pltpu.VMEM)
    return pl.pallas_call(
        sums_kernel,
        out_shape=jax.ShapeDtypeStruct((obs_index.shape[0], 8, cells), jnp.float32),
        in_specs=[pl.BlockSpec(memory_space=pltpu.SMEM)] + [vmem] * 3,
        out_specs=vmem,
        name="sums",
        compiler_params=pltpu.CompilerParams(vmem_limit_bytes=12 << 20),
        cost_estimate=pl.CostEstimate(flops=10**9, bytes_accessed=10**6, transcendentals=0),
    )(obs_count, obs_index, obs_value, obs_weight)


def by_tile(x):
    a, rows, lanes = x.shape
    x = x.reshape(a, rows // 8, 8, lanes // LANES, LANES)
    return jnp.swapaxes(x, 2, 3).reshape(-1, LANES)


def from_tiles(x, a, rows, lanes):
    x = x.reshape(a, rows // 8, lanes // LANES, 8, LANES)
    return jnp.swapaxes(x, 2, 3).reshape(a, rows, lanes)


def halves(x):
    lead = x.astype(jnp.bfloat16)
    return lead, (x - lead.astype(jnp.float32)).astype(jnp.bfloat16)


def cell_sums(indices, weights, values, cells):
    groups = cells // LANES
    group, lane = indices // LANES, indices % LANES
    row = lax.broadcasted_iota(jnp.int32, (2 * groups, indices.shape[1]), 0)
    both = jnp.where(row < groups, weights, weights * values)
    left = jnp.where(row % groups == group, both, 0.0)
    hit = lax.broadcasted_iota(jnp.int32, (LANES, indices.shape[1]), 0) == lane
    right = jnp.where(hit, 1.0, 0.0).astype(jnp.bfloat16)
    first = left.astype(jnp.bfloat16)
    rest = left - first.astype(jnp.float32)
    second = rest.astype(jnp.bfloat16)
    third = (rest - second.astype(jnp.float32)).astype(jnp.bfloat16)
    total = 0.0
    for part in (third, second, first):
        total += lax.dot_general(part, right, NT, preferred_element_type=jnp.float32)
    rows = [
        jnp.concatenate([total[s + g : s + g + 1] for g in range(groups)], axis=1)
        for s in (0, groups)
    ]
    return rows


def analysis_kernel(sums_ref, x_ref, out_ref, *scratch):
    patches = sums_ref.shape[0]
    members = x_ref.shape[0]
    cells = x_ref.shape[1] // patches
    matrix_ref, root_ref, spread_ref, left_ref, right_ref = scratch[:5]
    totals = [scratch[5 + 3 * b : 8 + 3 * b] for b in range(patches)]
    identity = jnp.where(
        lax.broadcasted_iota(jnp.int32, (members, members), 0)
        == lax.broadcasted_iota(jnp.int32, (members, members), 1),
        1.0,
        0.0,
    )
    each = range(patches)
    chunks = [pl.ds(c, members) for c in range(0, cells, members)]
    LEAD, REST = 0, 1

    def load(b, lead, rest, transpose=False):
        if lead is not None:
            pltpu.matmul_push_rhs(lead, LEAD, b, transpose=transpose)
        if rest is not None:
            pltpu.matmul_push_rhs(rest, REST, b, transpose=transpose)

    stream = lambda total, rows, use=None: pltpu.matmul_acc_lhs(total, rows, load_staged_rhs=use)

    def set_root(b, root):
        root_ref[b] = root
        left_ref[b, LEAD, :, :members], left_ref[b, REST, :, :members] = halves(root)

    means, projections, scales = [], [], []
    for b in each:
        x = x_ref[:, b * cells : (b + 1) * cells]
        mean = jnp.sum(x, axis=0, keepdims=True) * (1.0 / members)
        spread = x - mean
        weight_sum, value_sum = sums_ref[b, 0:1], sums_ref[b, 1:2]
        spread_ref[b, LEAD], spread_ref[b, REST] = halves(spread)
        left_ref[b, LEAD], left_ref[b, REST] = halves(spread * weight_sum)
        misfit = value_sum - weight_sum * mean
        projections.append(jnp.sum(spread * misfit, axis=1, keepdims=True))
        means.append(mean)
    for chunk in chunks:
        for b in each:
            load(b, spread_ref[b, LEAD, :, chunk], spread_ref[b, REST, :, chunk], transpose=True)
            stream(totals[b][0], left_ref[b, LEAD, :, chunk], LEAD)
            stream(totals[b][0], left_ref[b, REST, :, chunk])
            stream(totals[b][0], left_ref[b, LEAD, :, chunk], REST)
    for b in each:
        gram = pltpu.matmul_pop(totals[b][0]) + (members - 1.0) * identity
        scale = jnp.sqrt(jnp.sum(gram * gram, keepdims=True))
        scales.append(scale)
        start = gram * (1.0 / scale)
        matrix_ref[b] = start
        set_root(b, 1.5 * identity - 0.5 * start)
        right_ref[b, LEAD], right_ref[b, REST] = halves(start)

    def iterate(with_root):
        for b in each:
            load(b, right_ref[b, LEAD], right_ref[b, REST])
            stream(totals[b][0], right_ref[b, LEAD], LEAD)
            load(b, right_ref[b, LEAD], None)
            stream(totals[b][0], right_ref[b, REST])
            stream(totals[b][0], right_ref[b, LEAD], REST)
        squares = []
        for b in each:
            if with_root:
                stream(totals[b][2], left_ref[b, LEAD, :, :members])
            square = pltpu.matmul_pop(totals[b][0])
            lead, rest = halves(square)
            stream(totals[b][1], lead)
            stream(totals[b][1], lead, LEAD)
            stream(totals[b][1], rest)
            squares.append(square)
            if with_root:
                stream(totals[b][2], left_ref[b, LEAD, :, :members])
                stream(totals[b][2], left_ref[b, REST, :, :members])
        for b in each:
            cube = pltpu.matmul_pop(totals[b][1])
            matrix = 2.25 * matrix_ref[b] - 1.5 * squares[b] + 0.25 * cube
            matrix_ref[b] = matrix
            right_ref[b, LEAD], right_ref[b, REST] = halves(matrix)
        if with_root:
            for b in each:
                set_root(b, 1.5 * root_ref[b] - 0.5 * pltpu.matmul_pop(totals[b][2]))

    iterate(False)

    for _ in range(NS_ITERS - 2):
        iterate(True)
    roots = []
    for b in each:
        lead, rest = left_ref[b, LEAD, :, :members], left_ref[b, REST, :, :members]
        load(b, right_ref[b, LEAD], right_ref[b, REST])
        stream(totals[b][0], lead, LEAD)
        stream(totals[b][0], rest)
        stream(totals[b][0], lead, REST)
    for b in each:
        root = 1.5 * root_ref[b] - 0.5 * pltpu.matmul_pop(totals[b][0])
        root_ref[b] = root
        roots.append(halves(root))
    for c, chunk in enumerate(chunks):
        for b in each:
            load(b, spread_ref[b, LEAD, :, chunk], spread_ref[b, REST, :, chunk])
            stream(totals[b][c], roots[b][0], LEAD)
            stream(totals[b][c], roots[b][1])
            stream(totals[b][c], roots[b][0], REST)
    for b in each:
        along = jnp.sum(root_ref[b] * projections[b], axis=0, keepdims=True)
        mover = jnp.sum(root_ref[b] * along, axis=1, keepdims=True) / scales[b]
        gain = jnp.sqrt((members - 1.0) / scales[b])
        for c, chunk in enumerate(chunks):
            place = slice(b * cells + c * members, b * cells + (c + 1) * members)
            mean = means[b][:, c * members : (c + 1) * members]
            spread = x_ref[:, place] - mean
            shift = mean + jnp.sum(spread * mover, axis=0, keepdims=True)
            out_ref[:, place] = shift + gain * pltpu.matmul_pop(totals[b][c])


def analyse(arrived, sums):
    members, width = arrived.shape
    patches = sums.shape[0]
    cells = width // patches
    vmem = pl.BlockSpec(memory_space=pltpu.VMEM)
    square = (members, members)
    kernel = lambda *refs: pl.run_scoped(
        functools.partial(analysis_kernel, *refs),
        *(pltpu.ACC(b)(square, jnp.float32) for b in range(patches) for _ in range(3)),
    )
    return pl.pallas_call(
        kernel,
        out_shape=jax.ShapeDtypeStruct(arrived.shape, jnp.float32),
        in_specs=[vmem] * 2,
        out_specs=vmem,
        scratch_shapes=[
            pltpu.VMEM((patches, *square), jnp.float32),
            pltpu.VMEM((patches, *square), jnp.float32),
            pltpu.VMEM((patches, 2, members, cells), jnp.bfloat16),
            pltpu.VMEM((patches, 2, members, cells), jnp.bfloat16),
            pltpu.VMEM((patches, 2, *square), jnp.bfloat16),
        ],
        name="analysis",
        compiler_params=pltpu.CompilerParams(vmem_limit_bytes=16 << 20),
    )(sums, arrived)


def forecast(background_members, stencil_weight_table, devices, beside):
    members, rows, lons = background_members.shape
    width = rows * lons // devices
    vmem = pl.BlockSpec(memory_space=pltpu.VMEM)
    hbm = pl.BlockSpec(memory_space=pltpu.HBM)
    small = pltpu.CompilerParams(vmem_limit_bytes=12 << 20)
    packed = jax.ShapeDtypeStruct((members, 2 * lons + 5 * lons // members), jnp.float32)
    pair, cross = pl.pallas_call(
        edge_kernel,
        out_shape=[packed, packed],
        in_specs=[hbm] * 2,
        out_specs=[vmem] * 2,
        scratch_shapes=[
            pltpu.VMEM(background_members.shape, jnp.float32),
            pltpu.VMEM(stencil_weight_table.shape, jnp.float32),
            pltpu.SemaphoreType.DMA((2,)),
        ],
        name="edges",
        compiler_params=small,
    )(
        pltpu.with_memory_space_constraint(background_members, pltpu.HBM),
        pltpu.with_memory_space_constraint(stencil_weight_table, pltpu.HBM),
    )
    bands = lax.axis_size("lat")
    within = [(i, i ^ 1) for i in range(bands)]
    across = [(i, i - 1 + 2 * (i % 2)) for i in range(1, bands - 1)]
    cross = lax.ppermute(cross, "lat", across)
    pair = lax.ppermute(pair, "lat", within)
    middle, outer = pl.pallas_call(
        inner_kernel,
        out_shape=[
            jax.ShapeDtypeStruct((rows + 2, members, lons), jnp.float32),
            jax.ShapeDtypeStruct((4, members, lons), jnp.float32),
        ],
        in_specs=[vmem] * 2,
        out_specs=[vmem] * 2,
        scratch_shapes=[pltpu.VMEM((rows, members, lons), jnp.float32)],
        name="inner",
        compiler_params=small,
        cost_estimate=pl.CostEstimate(flops=10**9, bytes_accessed=4 * 10**6, transcendentals=0),
    )(by_tile(background_members), stencil_weight_table)
    middle, beside = lax.optimization_barrier((middle, beside))
    pieces = pl.pallas_call(
        stencil_kernel,
        out_shape=jax.ShapeDtypeStruct((devices, members, width), jnp.float32),
        in_specs=[vmem] * 5,
        out_specs=vmem,
        scratch_shapes=[
            pltpu.VMEM((2, 8, lons), jnp.float32),
            pltpu.VMEM((8, members, lons), jnp.float32),
            pltpu.VMEM((2, 4, members, lons), jnp.float32),
        ],
        name="stencil",
        compiler_params=small,
    )(middle, outer, stencil_weight_table, pair, cross)
    return pieces, beside


def body(background_members, stencil_weight_table, obs_index, obs_count, obs_value, obs_weight):
    member_slice, lat_rows, lon_cells = background_members.shape
    devices = lax.axis_size("mem")
    width = lat_rows * lon_cells // devices
    patches = obs_index.shape[1]
    sums = observation_sums(obs_index[0], obs_count, obs_value[0], obs_weight[0], width // patches)
    outgoing, sums = forecast(background_members, stencil_weight_table, devices, sums)
    arrived = lax.all_to_all(outgoing, "mem", split_axis=0, concat_axis=0, tiled=True)
    analysed = analyse(arrived.reshape(devices * member_slice, width), sums)
    returned = lax.all_to_all(
        analysed.reshape(devices, member_slice, width), "mem", split_axis=0, concat_axis=0, tiled=True
    )
    result = pl.pallas_call(
        functools.partial(return_kernel, lons=lon_cells),
        out_shape=jax.ShapeDtypeStruct((background_members.size // LANES, LANES), jnp.float32),
        in_specs=[pl.BlockSpec(memory_space=pltpu.VMEM)],
        out_specs=pl.BlockSpec(memory_space=pltpu.HBM),
        scratch_shapes=[
            pltpu.VMEM((background_members.size // LANES, LANES), jnp.float32),
            pltpu.SemaphoreType.DMA((member_slice,)),
        ],
        name="home",
        compiler_params=pltpu.CompilerParams(vmem_limit_bytes=12 << 20),
    )(by_tile(returned))
    return from_tiles(result, member_slice, lat_rows, lon_cells)


def solution(mesh):
    placed = (
        P("mem", "lat", None),
        P(None, "lat", None),
        P("lat", "mem", None),
        P("lat", "mem"),
        P("lat", "mem", None),
        P("lat", "mem", None),
    )
    return jax.shard_map(
        body, mesh=mesh, in_specs=placed, out_specs=P("mem", "lat", None), check_vma=False
    )
```

```python
import functools

import jax
import jax.numpy as jnp
from jax import lax
from jax.experimental import pallas as pl
from jax.experimental.pallas import tpu as pltpu
from jax.sharding import PartitionSpec as P


NS_ITERS = 8
LANES = 128
NT = (((1,), (1,)), ((), ()))


def edge_kernel(x_hbm, w_hbm, pair_ref, cross_ref, x_ref, w_ref, sems):
    copies = [
        pltpu.make_async_copy(x_hbm, x_ref, sems.at[0]),
        pltpu.make_async_copy(w_hbm, w_ref, sems.at[1]),
    ]
    for copy in copies:
        copy.start()
    for copy in copies:
        copy.wait()
    members, rows, lons = x_ref.shape
    even = lax.rem(lax.axis_index("lat"), 2) == 0

    def pack(out_ref, near, far):
        for k in range(members):
            out_ref[k : k + 1, :lons] = x_ref[k, near : near + 1]
            out_ref[k : k + 1, lons : 2 * lons] = x_ref[k, far : far + 1]
        for run in range(5 * lons // LANES):
            t, start = run // (lons // LANES), run % (lons // LANES) * LANES
            place = 2 * lons + run // members * LANES
            out_ref[run % members : run % members + 1, place : place + LANES] = w_ref[
                t, near : near + 1, start : start + LANES
            ]

    @pl.when(even)
    def _():
        pack(pair_ref, rows - 1, rows - 2)
        pack(cross_ref, 0, 1)

    @pl.when(jnp.logical_not(even))
    def _():
        pack(pair_ref, 0, 1)
        pack(cross_ref, rows - 1, rows - 2)


def step(src_ref, r, wide):
    lons = src_ref.shape[2]
    centre = src_ref[r]
    return (
        wide(0) * centre
        + wide(1) * src_ref[r - 1]
        + wide(2) * src_ref[r + 1]
        + wide(3) * pltpu.roll(centre, lons - 1, 1)
        + wide(4) * pltpu.roll(centre, 1, 1)
    )


def weights_of(w_ref, r, rows, members, tiles):
    def wide(t):
        start = (t * rows // 8 + r // 8) * tiles * 8 + r % 8
        return jnp.concatenate(
            [w_ref[pl.ds(start + 8 * j, members, stride=0), :] for j in range(tiles)], axis=1
        )

    return wide


def inner_kernel(
    x_ref, w_ref, count_hbm, index_hbm, value_hbm, weight_hbm,
    ready_ref, outer_ref, near_ref, sums_ref,
    field_ref, middle_ref, count_ref, index_ref, value_ref, weight_ref, sems,
):
    copies = [
        pltpu.make_async_copy(source, target, sems.at[i])
        for i, (source, target) in enumerate(
            (
                (count_hbm, count_ref),
                (index_hbm, index_ref),
                (value_hbm, value_ref),
                (weight_hbm, weight_ref),
            )
        )
    ]
    for copy in copies:
        copy.start()
    rows, members, lons = field_ref.shape
    half = ready_ref.shape[2]
    own = lambda r: weights_of(w_ref, r, rows, members, lons // LANES)
    part = 2 * LANES
    for block in range(0, rows, 8):
        for start in range(0, lons, part):
            field_ref[block : block + 8, :, start : start + part] = jnp.swapaxes(
                x_ref[:, block : block + 8, start : start + part], 0, 1
            )
    for place, r in enumerate((0, 1, rows - 2, rows - 1)):
        outer_ref[place] = field_ref[r]

    def first(r, carry):
        middle_ref[r] = step(field_ref, r, own(r))
        return carry

    def second(r, carry):
        done = step(middle_ref, r, own(r))
        for h in range(lons // half):
            ready_ref[(r - 2) * (lons // half) + h] = done[:, h * half : (h + 1) * half]
        return carry

    lax.fori_loop(1, rows - 1, first, 0)
    for place, r in enumerate((1, 2, rows - 3, rows - 2)):
        near_ref[place] = middle_ref[r]
    lax.fori_loop(2, rows - 2, second, 0)
    for copy in copies:
        copy.wait()
    slot = lax.broadcasted_iota(jnp.int32, (1, index_ref.shape[1]), 1)
    for b in range(index_ref.shape[0]):
        weights = jnp.where(slot < count_ref[0, b], weight_ref[b : b + 1, :], 0.0)
        weight_sum, value_sum = cell_sums(
            index_ref[b : b + 1, :], weights, value_ref[b : b + 1, :], sums_ref.shape[2]
        )
        sums_ref[b, 0:1] = weight_sum
        sums_ref[b, 1:2] = value_sum


def stencil_kernel(ready_ref, outer_ref, middle_in, w_ref, pair_ref, cross_ref, out_ref, side_ref, rim_ref, near_ref):
    members, lons = outer_ref.shape[1:]
    count, _, half = out_ref.shape
    rows = count * half // lons
    rim = 2 * (lons // half)
    out_ref[rim : count - rim] = ready_ref[...]
    even = lax.rem(lax.axis_index("lat"), 2) == 0

    def unpack(ref, near, far, side):
        rim_ref[near] = ref[:, :lons]
        rim_ref[far] = ref[:, lons : 2 * lons]
        for run in range(5 * lons // LANES):
            t, start = run // (lons // LANES), run % (lons // LANES) * LANES
            place = 2 * lons + run // members * LANES
            side_ref[side, t : t + 1, start : start + LANES] = ref[
                run % members : run % members + 1, place : place + LANES
            ]

    @pl.when(even)
    def _():
        unpack(pair_ref, 6, 7, 1)
        unpack(cross_ref, 1, 0, 0)

    @pl.when(jnp.logical_not(even))
    def _():
        unpack(pair_ref, 1, 0, 0)
        unpack(cross_ref, 6, 7, 1)

    for place in range(4):
        rim_ref[place + 2] = outer_ref[place]
    for side in range(2):
        for place in range(2):
            near_ref[side, 2 - 2 * side + place] = middle_in[2 * side + place]
    own = lambda r: weights_of(w_ref, r, rows, members, lons // LANES)
    beyond = lambda side: lambda t: jnp.broadcast_to(side_ref[side, t : t + 1], (members, lons))
    near_ref[0, 0] = step(rim_ref, 1, beyond(0))
    near_ref[0, 1] = step(rim_ref, 2, own(0))
    near_ref[1, 2] = step(rim_ref, 5, own(rows - 1))
    near_ref[1, 3] = step(rim_ref, 6, beyond(1))

    def put(r, done):
        for h in range(lons // half):
            out_ref[r * (lons // half) + h] = done[:, h * half : (h + 1) * half]

    for side, place, r in ((0, 1, 0), (0, 2, 1), (1, 1, rows - 2), (1, 2, rows - 1)):
        put(r, step(near_ref.at[side], place, own(r)))


def return_kernel(in_ref, out_hbm, field_ref, sems):
    rows, pieces, _, width = in_ref.shape
    part = 2 * LANES
    copies = []
    for block in range(0, rows, 8):
        for h in range(pieces):
            for start in range(0, width, part):
                field_ref[:, block : block + 8, h * width + start : h * width + start + part] = (
                    jnp.swapaxes(in_ref[block : block + 8, h, :, start : start + part], 0, 1)
                )
            place = (slice(None), pl.ds(block, 8), pl.ds(h * width, width))
            copies.append(
                pltpu.make_async_copy(field_ref.at[place], out_hbm.at[place], sems.at[len(copies)])
            )
            copies[-1].start()
    for copy in copies:
        copy.wait()


def by_tile(x):
    a, rows, lanes = x.shape
    x = x.reshape(a, rows // 8, 8, lanes // LANES, LANES)
    return jnp.swapaxes(x, 2, 3).reshape(-1, LANES)


def halves(x):
    lead = x.astype(jnp.bfloat16)
    return lead, (x - lead.astype(jnp.float32)).astype(jnp.bfloat16)


def cell_sums(indices, weights, values, cells):
    groups = cells // LANES
    group, lane = indices // LANES, indices % LANES
    row = lax.broadcasted_iota(jnp.int32, (2 * groups, indices.shape[1]), 0)
    both = jnp.where(row < groups, weights, weights * values)
    left = jnp.where(row % groups == group, both, 0.0)
    hit = lax.broadcasted_iota(jnp.int32, (LANES, indices.shape[1]), 0) == lane
    right = jnp.where(hit, 1.0, 0.0).astype(jnp.bfloat16)
    first = left.astype(jnp.bfloat16)
    rest = left - first.astype(jnp.float32)
    second = rest.astype(jnp.bfloat16)
    third = (rest - second.astype(jnp.float32)).astype(jnp.bfloat16)
    parts = jnp.concatenate([third, second, first], axis=0)
    dots = lax.dot_general(parts, right, NT, preferred_element_type=jnp.float32)
    height = 2 * groups
    total = (dots[:height] + dots[height : 2 * height]) + dots[2 * height :]
    rows = [
        jnp.concatenate([total[s + g : s + g + 1] for g in range(groups)], axis=1)
        for s in (0, groups)
    ]
    return rows


def analysis_kernel(sums_ref, x_ref, out_ref, *scratch):
    patches = sums_ref.shape[0]
    members = x_ref.shape[0]
    cells = x_ref.shape[1] // patches
    matrix_ref, root_ref, spread_ref, left_ref, right_ref = scratch[:5]
    totals = [scratch[5 + 3 * b : 8 + 3 * b] for b in range(patches)]
    identity = jnp.where(
        lax.broadcasted_iota(jnp.int32, (members, members), 0)
        == lax.broadcasted_iota(jnp.int32, (members, members), 1),
        1.0,
        0.0,
    )
    each = range(patches)
    chunks = [pl.ds(c, members) for c in range(0, cells, members)]
    LEAD, REST = 0, 1

    def load(b, lead, rest, transpose=False):
        if lead is not None:
            pltpu.matmul_push_rhs(lead, LEAD, b, transpose=transpose)
        if rest is not None:
            pltpu.matmul_push_rhs(rest, REST, b, transpose=transpose)

    stream = lambda total, rows, use=None: pltpu.matmul_acc_lhs(total, rows, load_staged_rhs=use)

    def set_root(b, root):
        root_ref[b] = root
        left_ref[b, LEAD, :, :members], left_ref[b, REST, :, :members] = halves(root)

    means, projections, scales = [], [], []
    for b in each:
        x = x_ref[:, b * cells : (b + 1) * cells]
        mean = jnp.sum(x, axis=0, keepdims=True) * (1.0 / members)
        spread = x - mean
        weight_sum, value_sum = sums_ref[b, 0:1], sums_ref[b, 1:2]
        spread_ref[b, LEAD], spread_ref[b, REST] = halves(spread)
        left_ref[b, LEAD], left_ref[b, REST] = halves(spread * weight_sum)
        misfit = value_sum - weight_sum * mean
        projections.append(jnp.sum(spread * misfit, axis=1, keepdims=True))
        means.append(mean)
    for chunk in chunks:
        for b in each:
            load(b, spread_ref[b, LEAD, :, chunk], spread_ref[b, REST, :, chunk], transpose=True)
            stream(totals[b][0], left_ref[b, LEAD, :, chunk], LEAD)
            stream(totals[b][0], left_ref[b, REST, :, chunk])
            stream(totals[b][0], left_ref[b, LEAD, :, chunk], REST)
    for b in each:
        gram = pltpu.matmul_pop(totals[b][0]) + (members - 1.0) * identity
        scale = jnp.sqrt(jnp.sum(gram * gram, keepdims=True))
        scales.append(scale)
        start = gram * (1.0 / scale)
        matrix_ref[b] = start
        set_root(b, 1.5 * identity - 0.5 * start)
        right_ref[b, LEAD], right_ref[b, REST] = halves(start)

    def iterate(with_root):
        for b in each:
            load(b, right_ref[b, LEAD], right_ref[b, REST])
            stream(totals[b][0], right_ref[b, LEAD], LEAD)
            load(b, right_ref[b, LEAD], None)
            stream(totals[b][0], right_ref[b, REST])
            stream(totals[b][0], right_ref[b, LEAD], REST)
        squares = []
        for b in each:
            if with_root:
                stream(totals[b][2], left_ref[b, LEAD, :, :members])
            square = pltpu.matmul_pop(totals[b][0])
            lead, rest = halves(square)
            stream(totals[b][1], lead)
            stream(totals[b][1], lead, LEAD)
            stream(totals[b][1], rest)
            squares.append(square)
            if with_root:
                stream(totals[b][2], left_ref[b, LEAD, :, :members])
                stream(totals[b][2], left_ref[b, REST, :, :members])
        for b in each:
            cube = pltpu.matmul_pop(totals[b][1])
            matrix = 2.25 * matrix_ref[b] - 1.5 * squares[b] + 0.25 * cube
            matrix_ref[b] = matrix
            right_ref[b, LEAD], right_ref[b, REST] = halves(matrix)
        if with_root:
            for b in each:
                set_root(b, 1.5 * root_ref[b] - 0.5 * pltpu.matmul_pop(totals[b][2]))

    iterate(False)

    for _ in range(NS_ITERS - 2):
        iterate(True)
    roots = []
    for b in each:
        lead, rest = left_ref[b, LEAD, :, :members], left_ref[b, REST, :, :members]
        load(b, right_ref[b, LEAD], right_ref[b, REST])
        stream(totals[b][0], lead, LEAD)
        stream(totals[b][0], rest)
        stream(totals[b][0], lead, REST)
    for b in each:
        root = 1.5 * root_ref[b] - 0.5 * pltpu.matmul_pop(totals[b][0])
        root_ref[b] = root
        roots.append(halves(root))
    for c, chunk in enumerate(chunks):
        for b in each:
            load(b, spread_ref[b, LEAD, :, chunk], spread_ref[b, REST, :, chunk])
            stream(totals[b][c], roots[b][0], LEAD)
            stream(totals[b][c], roots[b][1])
            stream(totals[b][c], roots[b][0], REST)
    for b in each:
        along = jnp.sum(root_ref[b] * projections[b], axis=0, keepdims=True)
        mover = jnp.sum(root_ref[b] * along, axis=1, keepdims=True) / scales[b]
        gain = jnp.sqrt((members - 1.0) / scales[b])
        for c, chunk in enumerate(chunks):
            place = slice(b * cells + c * members, b * cells + (c + 1) * members)
            mean = means[b][:, c * members : (c + 1) * members]
            spread = x_ref[:, place] - mean
            shift = mean + jnp.sum(spread * mover, axis=0, keepdims=True)
            out_ref[:, place] = shift + gain * pltpu.matmul_pop(totals[b][c])


def analyse(arrived, sums):
    members, width = arrived.shape
    patches = sums.shape[0]
    cells = width // patches
    vmem = pl.BlockSpec(memory_space=pltpu.VMEM)
    square = (members, members)
    kernel = lambda *refs: pl.run_scoped(
        functools.partial(analysis_kernel, *refs),
        *(pltpu.ACC(b)(square, jnp.float32) for b in range(patches) for _ in range(3)),
    )
    return pl.pallas_call(
        kernel,
        out_shape=jax.ShapeDtypeStruct(arrived.shape, jnp.float32),
        in_specs=[vmem] * 2,
        out_specs=vmem,
        scratch_shapes=[
            pltpu.VMEM((patches, *square), jnp.float32),
            pltpu.VMEM((patches, *square), jnp.float32),
            pltpu.VMEM((patches, 2, members, cells), jnp.bfloat16),
            pltpu.VMEM((patches, 2, members, cells), jnp.bfloat16),
            pltpu.VMEM((patches, 2, *square), jnp.bfloat16),
        ],
        name="analysis",
        compiler_params=pltpu.CompilerParams(vmem_limit_bytes=16 << 20),
    )(sums, arrived)


def forecast(background_members, stencil_weight_table, devices, observations):
    patches, slots = observations[1].shape
    in_hbm = lambda array: pltpu.with_memory_space_constraint(array, pltpu.HBM)
    members, rows, lons = background_members.shape
    width = rows * lons // devices
    vmem = pl.BlockSpec(memory_space=pltpu.VMEM)
    hbm = pl.BlockSpec(memory_space=pltpu.HBM)
    small = pltpu.CompilerParams(vmem_limit_bytes=12 << 20)
    packed = jax.ShapeDtypeStruct((members, 2 * lons + 5 * lons // members), jnp.float32)
    pair, cross = pl.pallas_call(
        edge_kernel,
        out_shape=[packed, packed],
        in_specs=[hbm] * 2,
        out_specs=[vmem] * 2,
        scratch_shapes=[
            pltpu.VMEM(background_members.shape, jnp.float32),
            pltpu.VMEM(stencil_weight_table.shape, jnp.float32),
            pltpu.SemaphoreType.DMA((2,)),
        ],
        name="edges",
        compiler_params=small,
    )(
        pltpu.with_memory_space_constraint(background_members, pltpu.HBM),
        pltpu.with_memory_space_constraint(stencil_weight_table, pltpu.HBM),
    )
    bands = lax.axis_size("lat")
    within = [(i, i ^ 1) for i in range(bands)]
    across = [(i, i - 1 + 2 * (i % 2)) for i in range(1, bands - 1)]
    cross = lax.ppermute(cross, "lat", across)
    pair = lax.ppermute(pair, "lat", within)
    ready, outer, middle, sums = pl.pallas_call(
        inner_kernel,
        out_shape=[
            jax.ShapeDtypeStruct((devices * (rows - 4) // rows, members, width), jnp.float32),
            jax.ShapeDtypeStruct((4, members, lons), jnp.float32),
            jax.ShapeDtypeStruct((4, members, lons), jnp.float32),
            jax.ShapeDtypeStruct((patches, 8, width // patches), jnp.float32),
        ],
        in_specs=[vmem] * 2 + [hbm] * 4,
        out_specs=[vmem] * 4,
        scratch_shapes=[pltpu.VMEM((rows, members, lons), jnp.float32)] * 2
        + [
            pltpu.SMEM((1, patches), jnp.int32),
            pltpu.VMEM((patches, slots), jnp.int32),
            pltpu.VMEM((patches, slots), jnp.float32),
            pltpu.VMEM((patches, slots), jnp.float32),
            pltpu.SemaphoreType.DMA((4,)),
        ],
        name="inner",
        compiler_params=small,
        cost_estimate=pl.CostEstimate(flops=10**9, bytes_accessed=4 * 10**6, transcendentals=0),
    )(background_members, by_tile(stencil_weight_table), *map(in_hbm, observations))
    pieces = pl.pallas_call(
        stencil_kernel,
        out_shape=jax.ShapeDtypeStruct((devices, members, width), jnp.float32),
        in_specs=[vmem] * 6,
        out_specs=vmem,
        scratch_shapes=[
            pltpu.VMEM((2, 8, lons), jnp.float32),
            pltpu.VMEM((8, members, lons), jnp.float32),
            pltpu.VMEM((2, 4, members, lons), jnp.float32),
        ],
        name="stencil",
        compiler_params=small,
    )(ready, outer, middle, by_tile(stencil_weight_table), pair, cross)
    return pieces, sums


def body(background_members, stencil_weight_table, obs_index, obs_count, obs_value, obs_weight):
    member_slice, lat_rows, lon_cells = background_members.shape
    devices = lax.axis_size("mem")
    width = lat_rows * lon_cells // devices
    observations = (obs_count, obs_index[0], obs_value[0], obs_weight[0])
    outgoing, sums = forecast(background_members, stencil_weight_table, devices, observations)
    arrived = lax.all_to_all(outgoing, "mem", split_axis=0, concat_axis=0, tiled=True)
    analysed = analyse(arrived.reshape(devices * member_slice, width), sums)
    returned = lax.all_to_all(
        analysed.reshape(devices, member_slice, width), "mem", split_axis=0, concat_axis=0, tiled=True
    )
    pieces = lon_cells // width
    return pl.pallas_call(
        return_kernel,
        out_shape=jax.ShapeDtypeStruct(background_members.shape, jnp.float32),
        in_specs=[pl.BlockSpec(memory_space=pltpu.VMEM)],
        out_specs=pl.BlockSpec(memory_space=pltpu.HBM),
        scratch_shapes=[
            pltpu.VMEM(background_members.shape, jnp.float32),
            pltpu.SemaphoreType.DMA((lat_rows // 8 * pieces,)),
        ],
        name="home",
        compiler_params=pltpu.CompilerParams(vmem_limit_bytes=12 << 20),
    )(returned.reshape(lat_rows, pieces, member_slice, width))


def solution(mesh):
    placed = (
        P("mem", "lat", None),
        P(None, "lat", None),
        P("lat", "mem", None),
        P("lat", "mem"),
        P("lat", "mem", None),
        P("lat", "mem", None),
    )
    return jax.shard_map(
        body, mesh=mesh, in_specs=placed, out_specs=P("mem", "lat", None), check_vma=False
    )
```

```python
import functools

import jax
import jax.numpy as jnp
from jax import lax
from jax.experimental import pallas as pl
from jax.experimental.pallas import tpu as pltpu
from jax.sharding import PartitionSpec as P


NS_ITERS = 8
LANES = 128
NT = (((1,), (1,)), ((), ()))


def edge_kernel(
    x_hbm, w_hbm, count_hbm, index_hbm, value_hbm, weight_hbm,
    pair_ref, cross_ref, sums_ref,
    x_ref, w_ref, count_ref, index_ref, value_ref, weight_ref, sems,
):
    fields = [
        pltpu.make_async_copy(x_hbm, x_ref, sems.at[4]),
        pltpu.make_async_copy(w_hbm, w_ref, sems.at[5]),
    ]
    copies = [
        pltpu.make_async_copy(source, target, sems.at[i])
        for i, (source, target) in enumerate(
            (
                (count_hbm, count_ref),
                (index_hbm, index_ref),
                (value_hbm, value_ref),
                (weight_hbm, weight_ref),
            )
        )
    ]
    for copy in copies:
        copy.start()
    for copy in fields:
        copy.start()
    for copy in copies:
        copy.wait()
    slot = lax.broadcasted_iota(jnp.int32, (1, index_ref.shape[1]), 1)
    for b in range(index_ref.shape[0]):
        weights = jnp.where(slot < count_ref[0, b], weight_ref[b : b + 1, :], 0.0)
        weight_sum, value_sum = cell_sums(
            index_ref[b : b + 1, :], weights, value_ref[b : b + 1, :], sums_ref.shape[2]
        )
        sums_ref[b, 0:1] = weight_sum
        sums_ref[b, 1:2] = value_sum
    for copy in fields:
        copy.wait()
    members, rows, lons = x_ref.shape
    even = lax.rem(lax.axis_index("lat"), 2) == 0

    def pack(out_ref, near, far):
        for k in range(members):
            out_ref[k : k + 1, :lons] = x_ref[k, near : near + 1]
            out_ref[k : k + 1, lons : 2 * lons] = x_ref[k, far : far + 1]
        for run in range(5 * lons // LANES):
            t, start = run // (lons // LANES), run % (lons // LANES) * LANES
            place = 2 * lons + run // members * LANES
            out_ref[run % members : run % members + 1, place : place + LANES] = w_ref[
                t, near : near + 1, start : start + LANES
            ]

    @pl.when(even)
    def _():
        pack(pair_ref, rows - 1, rows - 2)
        pack(cross_ref, 0, 1)

    @pl.when(jnp.logical_not(even))
    def _():
        pack(pair_ref, 0, 1)
        pack(cross_ref, rows - 1, rows - 2)


def step(src_ref, r, wide):
    lons = src_ref.shape[2]
    centre = src_ref[r]
    return (
        wide(0) * centre
        + wide(1) * src_ref[r - 1]
        + wide(2) * src_ref[r + 1]
        + wide(3) * pltpu.roll(centre, lons - 1, 1)
        + wide(4) * pltpu.roll(centre, 1, 1)
    )


def weights_of(w_ref, r, rows, members, tiles):
    def wide(t):
        start = (t * rows // 8 + r // 8) * tiles * 8 + r % 8
        return jnp.concatenate(
            [w_ref[pl.ds(start + 8 * j, members, stride=0), :] for j in range(tiles)], axis=1
        )

    return wide


def inner_kernel(x_ref, w_ref, ready_ref, outer_ref, near_ref, field_ref, middle_ref):
    rows, members, lons = field_ref.shape
    half = ready_ref.shape[2]
    own = lambda r: weights_of(w_ref, r, rows, members, lons // LANES)
    part = 2 * LANES
    for block in range(0, rows, 8):
        for start in range(0, lons, part):
            field_ref[block : block + 8, :, start : start + part] = jnp.swapaxes(
                x_ref[:, block : block + 8, start : start + part], 0, 1
            )
    for place, r in enumerate((0, 1, rows - 2, rows - 1)):
        outer_ref[place] = field_ref[r]

    def first(r, carry):
        middle_ref[r] = step(field_ref, r, own(r))
        return carry

    def second(r, carry):
        done = step(middle_ref, r, own(r))
        for h in range(lons // half):
            ready_ref[(r - 2) * (lons // half) + h] = done[:, h * half : (h + 1) * half]
        return carry

    lax.fori_loop(1, rows - 1, first, 0)
    for place, r in enumerate((1, 2, rows - 3, rows - 2)):
        near_ref[place] = middle_ref[r]
    lax.fori_loop(2, rows - 2, second, 0)


def stencil_kernel(ready_ref, outer_ref, middle_in, w_ref, pair_ref, cross_ref, out_ref, side_ref, rim_ref, near_ref):
    members, lons = outer_ref.shape[1:]
    count, _, half = out_ref.shape
    rows = count * half // lons
    rim = 2 * (lons // half)
    out_ref[rim : count - rim] = ready_ref[...]
    even = lax.rem(lax.axis_index("lat"), 2) == 0

    def unpack(ref, near, far, side):
        rim_ref[near] = ref[:, :lons]
        rim_ref[far] = ref[:, lons : 2 * lons]
        for run in range(5 * lons // LANES):
            t, start = run // (lons // LANES), run % (lons // LANES) * LANES
            place = 2 * lons + run // members * LANES
            side_ref[side, t : t + 1, start : start + LANES] = ref[
                run % members : run % members + 1, place : place + LANES
            ]

    @pl.when(even)
    def _():
        unpack(pair_ref, 6, 7, 1)
        unpack(cross_ref, 1, 0, 0)

    @pl.when(jnp.logical_not(even))
    def _():
        unpack(pair_ref, 1, 0, 0)
        unpack(cross_ref, 6, 7, 1)

    for place in range(4):
        rim_ref[place + 2] = outer_ref[place]
    for side in range(2):
        for place in range(2):
            near_ref[side, 2 - 2 * side + place] = middle_in[2 * side + place]
    own = lambda r: weights_of(w_ref, r, rows, members, lons // LANES)
    beyond = lambda side: lambda t: jnp.broadcast_to(side_ref[side, t : t + 1], (members, lons))
    near_ref[0, 0] = step(rim_ref, 1, beyond(0))
    near_ref[0, 1] = step(rim_ref, 2, own(0))
    near_ref[1, 2] = step(rim_ref, 5, own(rows - 1))
    near_ref[1, 3] = step(rim_ref, 6, beyond(1))

    def put(r, done):
        for h in range(lons // half):
            out_ref[r * (lons // half) + h] = done[:, h * half : (h + 1) * half]

    for side, place, r in ((0, 1, 0), (0, 2, 1), (1, 1, rows - 2), (1, 2, rows - 1)):
        put(r, step(near_ref.at[side], place, own(r)))


def return_kernel(in_ref, out_hbm, field_ref, sems):
    rows, pieces, _, width = in_ref.shape
    part = 2 * LANES
    copies = []
    for block in range(0, rows, 8):
        for h in range(pieces):
            for start in range(0, width, part):
                field_ref[:, block : block + 8, h * width + start : h * width + start + part] = (
                    jnp.swapaxes(in_ref[block : block + 8, h, :, start : start + part], 0, 1)
                )
            place = (slice(None), pl.ds(block, 8), pl.ds(h * width, width))
            copies.append(
                pltpu.make_async_copy(field_ref.at[place], out_hbm.at[place], sems.at[len(copies)])
            )
            copies[-1].start()
    for copy in copies:
        copy.wait()


def by_tile(x):
    a, rows, lanes = x.shape
    x = x.reshape(a, rows // 8, 8, lanes // LANES, LANES)
    return jnp.swapaxes(x, 2, 3).reshape(-1, LANES)


def halves(x):
    lead = x.astype(jnp.bfloat16)
    return lead, (x - lead.astype(jnp.float32)).astype(jnp.bfloat16)


def cell_sums(indices, weights, values, cells):
    groups = cells // LANES
    group, lane = indices // LANES, indices % LANES
    row = lax.broadcasted_iota(jnp.int32, (2 * groups, indices.shape[1]), 0)
    both = jnp.where(row < groups, weights, weights * values)
    left = jnp.where(row % groups == group, both, 0.0)
    hit = lax.broadcasted_iota(jnp.int32, (LANES, indices.shape[1]), 0) == lane
    right = jnp.where(hit, 1.0, 0.0).astype(jnp.bfloat16)
    first = left.astype(jnp.bfloat16)
    rest = left - first.astype(jnp.float32)
    second = rest.astype(jnp.bfloat16)
    third = (rest - second.astype(jnp.float32)).astype(jnp.bfloat16)
    parts = jnp.concatenate([third, second, first], axis=0)
    dots = lax.dot_general(parts, right, NT, preferred_element_type=jnp.float32)
    height = 2 * groups
    total = (dots[:height] + dots[height : 2 * height]) + dots[2 * height :]
    rows = [
        jnp.concatenate([total[s + g : s + g + 1] for g in range(groups)], axis=1)
        for s in (0, groups)
    ]
    return rows


def analysis_kernel(sums_ref, x_ref, out_ref, *scratch):
    patches = sums_ref.shape[0]
    members = x_ref.shape[0]
    cells = x_ref.shape[1] // patches
    matrix_ref, root_ref, spread_ref, left_ref, right_ref = scratch[:5]
    totals = [scratch[5 + 3 * b : 8 + 3 * b] for b in range(patches)]
    identity = jnp.where(
        lax.broadcasted_iota(jnp.int32, (members, members), 0)
        == lax.broadcasted_iota(jnp.int32, (members, members), 1),
        1.0,
        0.0,
    )
    each = range(patches)
    chunks = [pl.ds(c, members) for c in range(0, cells, members)]
    LEAD, REST = 0, 1

    def load(b, lead, rest, transpose=False):
        if lead is not None:
            pltpu.matmul_push_rhs(lead, LEAD, b, transpose=transpose)
        if rest is not None:
            pltpu.matmul_push_rhs(rest, REST, b, transpose=transpose)

    stream = lambda total, rows, use=None: pltpu.matmul_acc_lhs(total, rows, load_staged_rhs=use)

    def set_root(b, root):
        root_ref[b] = root
        left_ref[b, LEAD, :, :members], left_ref[b, REST, :, :members] = halves(root)

    means, projections, scales = [], [], []
    for b in each:
        x = x_ref[:, b * cells : (b + 1) * cells]
        mean = jnp.sum(x, axis=0, keepdims=True) * (1.0 / members)
        spread = x - mean
        weight_sum, value_sum = sums_ref[b, 0:1], sums_ref[b, 1:2]
        spread_ref[b, LEAD], spread_ref[b, REST] = halves(spread)
        left_ref[b, LEAD], left_ref[b, REST] = halves(spread * weight_sum)
        misfit = value_sum - weight_sum * mean
        projections.append(jnp.sum(spread * misfit, axis=1, keepdims=True))
        means.append(mean)
    for chunk in chunks:
        for b in each:
            load(b, spread_ref[b, LEAD, :, chunk], spread_ref[b, REST, :, chunk], transpose=True)
            stream(totals[b][0], left_ref[b, LEAD, :, chunk], LEAD)
            stream(totals[b][0], left_ref[b, REST, :, chunk])
            stream(totals[b][0], left_ref[b, LEAD, :, chunk], REST)
    for b in each:
        gram = pltpu.matmul_pop(totals[b][0]) + (members - 1.0) * identity
        scale = jnp.sqrt(jnp.sum(gram * gram, keepdims=True))
        scales.append(scale)
        start = gram * (1.0 / scale)
        start = 0.5 * start
        matrix_ref[b] = start
        set_root(b, 1.5 * identity - start)
        right_ref[b, LEAD], right_ref[b, REST] = halves(start)

    def open_step(b):
        load(b, right_ref[b, LEAD], right_ref[b, REST])
        stream(totals[b][0], right_ref[b, LEAD], LEAD)
        load(b, right_ref[b, LEAD], None)
        stream(totals[b][0], right_ref[b, REST])
        stream(totals[b][0], right_ref[b, LEAD], REST)

    def close_step(b, with_root):
        if with_root:
            stream(totals[b][2], left_ref[b, LEAD, :, :members])
        factor = (2.25 * identity - 3.0 * matrix_ref[b]) + pltpu.matmul_pop(totals[b][0])
        lead, rest = halves(factor)
        stream(totals[b][1], lead)
        stream(totals[b][1], lead, LEAD)
        stream(totals[b][1], rest)
        if with_root:
            stream(totals[b][2], left_ref[b, LEAD, :, :members])
            stream(totals[b][2], left_ref[b, REST, :, :members])
        matrix = pltpu.matmul_pop(totals[b][1])
        matrix_ref[b] = matrix
        right_ref[b, LEAD], right_ref[b, REST] = halves(matrix)
        if with_root:
            set_root(b, 1.5 * root_ref[b] - pltpu.matmul_pop(totals[b][2]))

    for k in range(NS_ITERS - 1):
        for b in each:
            open_step(b)
        for b in each:
            close_step(b, k > 0)
    roots = []
    for b in each:
        load(b, right_ref[b, LEAD], right_ref[b, REST])
        lead, rest = left_ref[b, LEAD, :, :members], left_ref[b, REST, :, :members]
        stream(totals[b][0], lead, LEAD)
        stream(totals[b][0], rest)
        stream(totals[b][0], lead, REST)
    for b in each:
        root = 1.5 * root_ref[b] - pltpu.matmul_pop(totals[b][0])
        root_ref[b] = root
        roots.append(halves(root))
    for c, chunk in enumerate(chunks):
        for b in each:
            load(b, spread_ref[b, LEAD, :, chunk], spread_ref[b, REST, :, chunk])
            stream(totals[b][c], roots[b][0], LEAD)
            stream(totals[b][c], roots[b][1])
            stream(totals[b][c], roots[b][0], REST)
    for b in each:
        along = jnp.sum(root_ref[b] * projections[b], axis=0, keepdims=True)
        mover = jnp.sum(root_ref[b] * along, axis=1, keepdims=True) / scales[b]
        gain = jnp.sqrt((members - 1.0) / scales[b])
        for c, chunk in enumerate(chunks):
            place = slice(b * cells + c * members, b * cells + (c + 1) * members)
            mean = means[b][:, c * members : (c + 1) * members]
            spread = x_ref[:, place] - mean
            shift = mean + jnp.sum(spread * mover, axis=0, keepdims=True)
            out_ref[:, place] = shift + gain * pltpu.matmul_pop(totals[b][c])


def analyse(arrived, sums):
    members, width = arrived.shape
    patches = sums.shape[0]
    cells = width // patches
    vmem = pl.BlockSpec(memory_space=pltpu.VMEM)
    square = (members, members)
    kernel = lambda *refs: pl.run_scoped(
        functools.partial(analysis_kernel, *refs),
        *(pltpu.ACC(b)(square, jnp.float32) for b in range(patches) for _ in range(3)),
    )
    return pl.pallas_call(
        kernel,
        out_shape=jax.ShapeDtypeStruct(arrived.shape, jnp.float32),
        in_specs=[vmem] * 2,
        out_specs=vmem,
        scratch_shapes=[
            pltpu.VMEM((patches, *square), jnp.float32),
            pltpu.VMEM((patches, *square), jnp.float32),
            pltpu.VMEM((patches, 2, members, cells), jnp.bfloat16),
            pltpu.VMEM((patches, 2, members, cells), jnp.bfloat16),
            pltpu.VMEM((patches, 2, *square), jnp.bfloat16),
        ],
        name="analysis",
        compiler_params=pltpu.CompilerParams(vmem_limit_bytes=16 << 20),
    )(sums, arrived)


def forecast(background_members, stencil_weight_table, devices, observations):
    patches, slots = observations[1].shape
    in_hbm = lambda array: pltpu.with_memory_space_constraint(array, pltpu.HBM)
    members, rows, lons = background_members.shape
    width = rows * lons // devices
    vmem = pl.BlockSpec(memory_space=pltpu.VMEM)
    hbm = pl.BlockSpec(memory_space=pltpu.HBM)
    small = pltpu.CompilerParams(vmem_limit_bytes=12 << 20)
    packed = jax.ShapeDtypeStruct((members, 2 * lons + 5 * lons // members), jnp.float32)
    pair, cross, sums = pl.pallas_call(
        edge_kernel,
        out_shape=[
            packed,
            packed,
            jax.ShapeDtypeStruct((patches, 8, width // patches), jnp.float32),
        ],
        in_specs=[hbm] * 6,
        out_specs=[vmem] * 3,
        scratch_shapes=[
            pltpu.VMEM(background_members.shape, jnp.float32),
            pltpu.VMEM(stencil_weight_table.shape, jnp.float32),
            pltpu.SMEM((1, patches), jnp.int32),
            pltpu.VMEM((patches, slots), jnp.int32),
            pltpu.VMEM((patches, slots), jnp.float32),
            pltpu.VMEM((patches, slots), jnp.float32),
            pltpu.SemaphoreType.DMA((6,)),
        ],
        name="edges",
        compiler_params=small,
    )(*map(in_hbm, (background_members, stencil_weight_table, *observations)))
    bands = lax.axis_size("lat")
    within = [(i, i ^ 1) for i in range(bands)]
    across = [(i, i - 1 + 2 * (i % 2)) for i in range(1, bands - 1)]
    cross = lax.ppermute(cross, "lat", across)
    pair = lax.ppermute(pair, "lat", within)
    ready, outer, middle = pl.pallas_call(
        inner_kernel,
        out_shape=[
            jax.ShapeDtypeStruct((devices * (rows - 4) // rows, members, width), jnp.float32),
            jax.ShapeDtypeStruct((4, members, lons), jnp.float32),
            jax.ShapeDtypeStruct((4, members, lons), jnp.float32),
        ],
        in_specs=[vmem] * 2,
        out_specs=[vmem] * 3,
        scratch_shapes=[pltpu.VMEM((rows, members, lons), jnp.float32)] * 2,
        name="inner",
        compiler_params=small,
        cost_estimate=pl.CostEstimate(flops=10**9, bytes_accessed=4 * 10**6, transcendentals=0),
    )(background_members, by_tile(stencil_weight_table))
    pieces = pl.pallas_call(
        stencil_kernel,
        out_shape=jax.ShapeDtypeStruct((devices, members, width), jnp.float32),
        in_specs=[vmem] * 6,
        out_specs=vmem,
        scratch_shapes=[
            pltpu.VMEM((2, 8, lons), jnp.float32),
            pltpu.VMEM((8, members, lons), jnp.float32),
            pltpu.VMEM((2, 4, members, lons), jnp.float32),
        ],
        name="stencil",
        compiler_params=small,
    )(ready, outer, middle, by_tile(stencil_weight_table), pair, cross)
    return pieces, sums


def body(background_members, stencil_weight_table, obs_index, obs_count, obs_value, obs_weight):
    member_slice, lat_rows, lon_cells = background_members.shape
    devices = lax.axis_size("mem")
    width = lat_rows * lon_cells // devices
    observations = (obs_count, obs_index[0], obs_value[0], obs_weight[0])
    outgoing, sums = forecast(background_members, stencil_weight_table, devices, observations)
    arrived = lax.all_to_all(outgoing, "mem", split_axis=0, concat_axis=0, tiled=True)
    analysed = analyse(arrived.reshape(devices * member_slice, width), sums)
    returned = lax.all_to_all(
        analysed.reshape(devices, member_slice, width), "mem", split_axis=0, concat_axis=0, tiled=True
    )
    pieces = lon_cells // width
    return pl.pallas_call(
        return_kernel,
        out_shape=jax.ShapeDtypeStruct(background_members.shape, jnp.float32),
        in_specs=[pl.BlockSpec(memory_space=pltpu.VMEM)],
        out_specs=pl.BlockSpec(memory_space=pltpu.HBM),
        scratch_shapes=[
            pltpu.VMEM(background_members.shape, jnp.float32),
            pltpu.SemaphoreType.DMA((lat_rows // 8 * pieces,)),
        ],
        name="home",
        compiler_params=pltpu.CompilerParams(vmem_limit_bytes=12 << 20),
    )(returned.reshape(lat_rows, pieces, member_slice, width))


def solution(mesh):
    placed = (
        P("mem", "lat", None),
        P(None, "lat", None),
        P("lat", "mem", None),
        P("lat", "mem"),
        P("lat", "mem", None),
        P("lat", "mem", None),
    )
    return jax.shard_map(
        body, mesh=mesh, in_specs=placed, out_specs=P("mem", "lat", None), check_vma=False
    )
```

```python
import functools

import jax
import jax.numpy as jnp
from jax import lax
from jax.experimental import pallas as pl
from jax.experimental.pallas import tpu as pltpu
from jax.sharding import PartitionSpec as P


NS_ITERS = 8
LANES = 128
NT = (((1,), (1,)), ((), ()))


def edge_kernel(x_hbm, w_hbm, pair_ref, cross_ref, x_ref, w_ref, sems):
    copies = [
        pltpu.make_async_copy(x_hbm, x_ref, sems.at[0]),
        pltpu.make_async_copy(w_hbm, w_ref, sems.at[1]),
    ]
    for copy in copies:
        copy.start()
    for copy in copies:
        copy.wait()
    members, rows, lons = x_ref.shape
    even = lax.rem(lax.axis_index("lat"), 2) == 0

    def pack(out_ref, near, far):
        for k in range(members):
            out_ref[k : k + 1, :lons] = x_ref[k, near : near + 1]
            out_ref[k : k + 1, lons : 2 * lons] = x_ref[k, far : far + 1]
        for run in range(5 * lons // LANES):
            t, start = run // (lons // LANES), run % (lons // LANES) * LANES
            place = 2 * lons + run // members * LANES
            out_ref[run % members : run % members + 1, place : place + LANES] = w_ref[
                t, near : near + 1, start : start + LANES
            ]

    @pl.when(even)
    def _():
        pack(pair_ref, rows - 1, rows - 2)
        pack(cross_ref, 0, 1)

    @pl.when(jnp.logical_not(even))
    def _():
        pack(pair_ref, 0, 1)
        pack(cross_ref, rows - 1, rows - 2)


def step(src_ref, r, wide):
    lons = src_ref.shape[2]
    centre = src_ref[r]
    return (
        wide(0) * centre
        + wide(1) * src_ref[r - 1]
        + wide(2) * src_ref[r + 1]
        + wide(3) * pltpu.roll(centre, lons - 1, 1)
        + wide(4) * pltpu.roll(centre, 1, 1)
    )


def weights_of(w_ref, r, rows, members, tiles):
    def wide(t):
        start = (t * rows // 8 + r // 8) * tiles * 8 + r % 8
        return jnp.concatenate(
            [w_ref[pl.ds(start + 8 * j, members, stride=0), :] for j in range(tiles)], axis=1
        )

    return wide


def inner_kernel(
    x_ref, w_ref, count_hbm, index_hbm, value_hbm, weight_hbm,
    ready_ref, outer_ref, near_ref, sums_ref,
    field_ref, middle_ref, count_ref, index_ref, value_ref, weight_ref, sems,
):
    copies = [
        pltpu.make_async_copy(source, target, sems.at[i])
        for i, (source, target) in enumerate(
            (
                (count_hbm, count_ref),
                (index_hbm, index_ref),
                (value_hbm, value_ref),
                (weight_hbm, weight_ref),
            )
        )
    ]
    for copy in copies:
        copy.start()
    rows, members, lons = field_ref.shape
    half = ready_ref.shape[2]
    own = lambda r: weights_of(w_ref, r, rows, members, lons // LANES)
    part = 2 * LANES
    for block in range(0, rows, 8):
        for start in range(0, lons, part):
            field_ref[block : block + 8, :, start : start + part] = jnp.swapaxes(
                x_ref[:, block : block + 8, start : start + part], 0, 1
            )
    for place, r in enumerate((0, 1, rows - 2, rows - 1)):
        outer_ref[place] = field_ref[r]

    def first(r, carry):
        middle_ref[r] = step(field_ref, r, own(r))
        return carry

    def second(r, carry):
        done = step(middle_ref, r, own(r))
        for h in range(lons // half):
            ready_ref[(r - 2) * (lons // half) + h] = done[:, h * half : (h + 1) * half]
        return carry

    lax.fori_loop(1, rows - 1, first, 0, unroll=2)
    for place, r in enumerate((1, 2, rows - 3, rows - 2)):
        near_ref[place] = middle_ref[r]
    lax.fori_loop(2, rows - 2, second, 0, unroll=2)
    for copy in copies:
        copy.wait()
    slot = lax.broadcasted_iota(jnp.int32, (1, index_ref.shape[1]), 1)
    for b in range(index_ref.shape[0]):
        weights = jnp.where(slot < count_ref[0, b], weight_ref[b : b + 1, :], 0.0)
        weight_sum, value_sum = cell_sums(
            index_ref[b : b + 1, :], weights, value_ref[b : b + 1, :], sums_ref.shape[2]
        )
        sums_ref[b, 0:1] = weight_sum
        sums_ref[b, 1:2] = value_sum


def stencil_kernel(ready_ref, outer_ref, middle_in, w_ref, pair_ref, cross_ref, out_ref, side_ref, rim_ref, near_ref):
    members, lons = outer_ref.shape[1:]
    count, _, half = out_ref.shape
    rows = count * half // lons
    rim = 2 * (lons // half)
    out_ref[rim : count - rim] = ready_ref[...]
    even = lax.rem(lax.axis_index("lat"), 2) == 0

    def unpack(ref, near, far, side):
        rim_ref[near] = ref[:, :lons]
        rim_ref[far] = ref[:, lons : 2 * lons]
        for run in range(5 * lons // LANES):
            t, start = run // (lons // LANES), run % (lons // LANES) * LANES
            place = 2 * lons + run // members * LANES
            side_ref[side, t : t + 1, start : start + LANES] = ref[
                run % members : run % members + 1, place : place + LANES
            ]

    @pl.when(even)
    def _():
        unpack(pair_ref, 6, 7, 1)
        unpack(cross_ref, 1, 0, 0)

    @pl.when(jnp.logical_not(even))
    def _():
        unpack(pair_ref, 1, 0, 0)
        unpack(cross_ref, 6, 7, 1)

    for place in range(4):
        rim_ref[place + 2] = outer_ref[place]
    for side in range(2):
        for place in range(2):
            near_ref[side, 2 - 2 * side + place] = middle_in[2 * side + place]
    own = lambda r: weights_of(w_ref, r, rows, members, lons // LANES)
    beyond = lambda side: lambda t: jnp.broadcast_to(side_ref[side, t : t + 1], (members, lons))
    near_ref[0, 0] = step(rim_ref, 1, beyond(0))
    near_ref[0, 1] = step(rim_ref, 2, own(0))
    near_ref[1, 2] = step(rim_ref, 5, own(rows - 1))
    near_ref[1, 3] = step(rim_ref, 6, beyond(1))

    def put(r, done):
        for h in range(lons // half):
            out_ref[r * (lons // half) + h] = done[:, h * half : (h + 1) * half]

    for side, place, r in ((0, 1, 0), (0, 2, 1), (1, 1, rows - 2), (1, 2, rows - 1)):
        put(r, step(near_ref.at[side], place, own(r)))


def return_kernel(in_ref, out_hbm, field_ref, sems):
    rows, pieces, _, width = in_ref.shape
    part = 2 * LANES
    copies = []
    for block in range(0, rows, 8):
        for h in range(pieces):
            for start in range(0, width, part):
                field_ref[:, block : block + 8, h * width + start : h * width + start + part] = (
                    jnp.swapaxes(in_ref[block : block + 8, h, :, start : start + part], 0, 1)
                )
            place = (slice(None), pl.ds(block, 8), pl.ds(h * width, width))
            copies.append(
                pltpu.make_async_copy(field_ref.at[place], out_hbm.at[place], sems.at[len(copies)])
            )
            copies[-1].start()
    for copy in copies:
        copy.wait()


def by_tile(x):
    a, rows, lanes = x.shape
    x = x.reshape(a, rows // 8, 8, lanes // LANES, LANES)
    return jnp.swapaxes(x, 2, 3).reshape(-1, LANES)


def halves(x):
    lead = x.astype(jnp.bfloat16)
    return lead, (x - lead.astype(jnp.float32)).astype(jnp.bfloat16)


def cell_sums(indices, weights, values, cells):
    groups = cells // LANES
    group, lane = indices // LANES, indices % LANES
    row = lax.broadcasted_iota(jnp.int32, (2 * groups, indices.shape[1]), 0)
    both = jnp.where(row < groups, weights, weights * values)
    left = jnp.where(row % groups == group, both, 0.0)
    hit = lax.broadcasted_iota(jnp.int32, (LANES, indices.shape[1]), 0) == lane
    right = jnp.where(hit, 1.0, 0.0).astype(jnp.bfloat16)
    first = left.astype(jnp.bfloat16)
    rest = left - first.astype(jnp.float32)
    second = rest.astype(jnp.bfloat16)
    third = (rest - second.astype(jnp.float32)).astype(jnp.bfloat16)
    parts = jnp.concatenate([third, second, first], axis=0)
    dots = lax.dot_general(parts, right, NT, preferred_element_type=jnp.float32)
    height = 2 * groups
    total = (dots[:height] + dots[height : 2 * height]) + dots[2 * height :]
    rows = [
        jnp.concatenate([total[s + g : s + g + 1] for g in range(groups)], axis=1)
        for s in (0, groups)
    ]
    return rows


def analysis_kernel(sums_ref, x_ref, out_ref, *scratch):
    patches = sums_ref.shape[0]
    members = x_ref.shape[0]
    cells = x_ref.shape[1] // patches
    matrix_ref, root_ref, spread_ref, left_ref, right_ref = scratch[:5]
    totals = [scratch[5 + 3 * b : 8 + 3 * b] for b in range(patches)]
    identity = jnp.where(
        lax.broadcasted_iota(jnp.int32, (members, members), 0)
        == lax.broadcasted_iota(jnp.int32, (members, members), 1),
        1.0,
        0.0,
    )
    each = range(patches)
    chunks = [pl.ds(c, members) for c in range(0, cells, members)]
    LEAD, REST = 0, 1

    def load(b, lead, rest, transpose=False):
        if lead is not None:
            pltpu.matmul_push_rhs(lead, LEAD, b, transpose=transpose)
        if rest is not None:
            pltpu.matmul_push_rhs(rest, REST, b, transpose=transpose)

    stream = lambda total, rows, use=None: pltpu.matmul_acc_lhs(total, rows, load_staged_rhs=use)

    def set_root(b, root):
        root_ref[b] = root
        left_ref[b, LEAD, :, :members], left_ref[b, REST, :, :members] = halves(root)

    means, projections, scales = [], [], []
    for b in each:
        x = x_ref[:, b * cells : (b + 1) * cells]
        mean = jnp.sum(x, axis=0, keepdims=True) * (1.0 / members)
        spread = x - mean
        weight_sum, value_sum = sums_ref[b, 0:1], sums_ref[b, 1:2]
        spread_ref[b, LEAD], spread_ref[b, REST] = halves(spread)
        left_ref[b, LEAD], left_ref[b, REST] = halves(spread * weight_sum)
        misfit = value_sum - weight_sum * mean
        projections.append(jnp.sum(spread * misfit, axis=1, keepdims=True))
        means.append(mean)
    for chunk in chunks:
        for b in each:
            load(b, spread_ref[b, LEAD, :, chunk], spread_ref[b, REST, :, chunk], transpose=True)
            stream(totals[b][0], left_ref[b, LEAD, :, chunk], LEAD)
            stream(totals[b][0], left_ref[b, REST, :, chunk])
            stream(totals[b][0], left_ref[b, LEAD, :, chunk], REST)
    for b in each:
        gram = pltpu.matmul_pop(totals[b][0]) + (members - 1.0) * identity
        scale = jnp.sqrt(jnp.sum(gram * gram, keepdims=True))
        scales.append(scale)
        start = gram * (1.0 / scale)
        start = 0.5 * start
        matrix_ref[b] = start
        set_root(b, 1.5 * identity - start)
        right_ref[b, LEAD], right_ref[b, REST] = halves(start)

    def open_step(b):
        load(b, right_ref[b, LEAD], right_ref[b, REST])
        stream(totals[b][0], right_ref[b, LEAD], LEAD)
        load(b, right_ref[b, LEAD], None)
        stream(totals[b][0], right_ref[b, REST])
        stream(totals[b][0], right_ref[b, LEAD], REST)

    def close_step(b, with_root):
        if with_root:
            stream(totals[b][2], left_ref[b, LEAD, :, :members])
        factor = (2.25 * identity - 3.0 * matrix_ref[b]) + pltpu.matmul_pop(totals[b][0])
        lead, rest = halves(factor)
        stream(totals[b][1], lead)
        stream(totals[b][1], lead, LEAD)
        stream(totals[b][1], rest)
        if with_root:
            stream(totals[b][2], left_ref[b, LEAD, :, :members])
            stream(totals[b][2], left_ref[b, REST, :, :members])
        matrix = pltpu.matmul_pop(totals[b][1])
        matrix_ref[b] = matrix
        right_ref[b, LEAD], right_ref[b, REST] = halves(matrix)
        if with_root:
            set_root(b, 1.5 * root_ref[b] - pltpu.matmul_pop(totals[b][2]))

    for k in range(NS_ITERS - 1):
        for b in each:
            open_step(b)
        for b in each:
            close_step(b, k > 0)
    roots = []
    for b in each:
        load(b, right_ref[b, LEAD], right_ref[b, REST])
        lead, rest = left_ref[b, LEAD, :, :members], left_ref[b, REST, :, :members]
        stream(totals[b][0], lead, LEAD)
        stream(totals[b][0], rest)
        stream(totals[b][0], lead, REST)
    for b in each:
        root = 1.5 * root_ref[b] - pltpu.matmul_pop(totals[b][0])
        root_ref[b] = root
        roots.append(halves(root))
    for c, chunk in enumerate(chunks):
        for b in each:
            load(b, spread_ref[b, LEAD, :, chunk], spread_ref[b, REST, :, chunk])
            stream(totals[b][c], roots[b][0], LEAD)
            stream(totals[b][c], roots[b][1])
            stream(totals[b][c], roots[b][0], REST)
    for b in each:
        along = jnp.sum(root_ref[b] * projections[b], axis=0, keepdims=True)
        mover = jnp.sum(root_ref[b] * along, axis=1, keepdims=True) / scales[b]
        gain = jnp.sqrt((members - 1.0) / scales[b])
        for c, chunk in enumerate(chunks):
            place = slice(b * cells + c * members, b * cells + (c + 1) * members)
            mean = means[b][:, c * members : (c + 1) * members]
            spread = x_ref[:, place] - mean
            shift = mean + jnp.sum(spread * mover, axis=0, keepdims=True)
            out_ref[:, place] = shift + gain * pltpu.matmul_pop(totals[b][c])


def analyse(arrived, sums):
    members, width = arrived.shape
    patches = sums.shape[0]
    cells = width // patches
    vmem = pl.BlockSpec(memory_space=pltpu.VMEM)
    square = (members, members)
    kernel = lambda *refs: pl.run_scoped(
        functools.partial(analysis_kernel, *refs),
        *(pltpu.ACC(b)(square, jnp.float32) for b in range(patches) for _ in range(3)),
    )
    return pl.pallas_call(
        kernel,
        out_shape=jax.ShapeDtypeStruct(arrived.shape, jnp.float32),
        in_specs=[vmem] * 2,
        out_specs=vmem,
        scratch_shapes=[
            pltpu.VMEM((patches, *square), jnp.float32),
            pltpu.VMEM((patches, *square), jnp.float32),
            pltpu.VMEM((patches, 2, members, cells), jnp.bfloat16),
            pltpu.VMEM((patches, 2, members, cells), jnp.bfloat16),
            pltpu.VMEM((patches, 2, *square), jnp.bfloat16),
        ],
        name="analysis",
        compiler_params=pltpu.CompilerParams(vmem_limit_bytes=16 << 20),
    )(sums, arrived)


def forecast(background_members, stencil_weight_table, devices, observations):
    patches, slots = observations[1].shape
    in_hbm = lambda array: pltpu.with_memory_space_constraint(array, pltpu.HBM)
    members, rows, lons = background_members.shape
    width = rows * lons // devices
    vmem = pl.BlockSpec(memory_space=pltpu.VMEM)
    hbm = pl.BlockSpec(memory_space=pltpu.HBM)
    small = pltpu.CompilerParams(vmem_limit_bytes=12 << 20)
    packed = jax.ShapeDtypeStruct((members, 2 * lons + 5 * lons // members), jnp.float32)
    pair, cross = pl.pallas_call(
        edge_kernel,
        out_shape=[packed, packed],
        in_specs=[hbm] * 2,
        out_specs=[vmem] * 2,
        scratch_shapes=[
            pltpu.VMEM(background_members.shape, jnp.float32),
            pltpu.VMEM(stencil_weight_table.shape, jnp.float32),
            pltpu.SemaphoreType.DMA((2,)),
        ],
        name="edges",
        compiler_params=small,
    )(
        pltpu.with_memory_space_constraint(background_members, pltpu.HBM),
        pltpu.with_memory_space_constraint(stencil_weight_table, pltpu.HBM),
    )
    bands = lax.axis_size("lat")
    within = [(i, i ^ 1) for i in range(bands)]
    across = [(i, i - 1 + 2 * (i % 2)) for i in range(1, bands - 1)]
    cross = lax.ppermute(cross, "lat", across)
    pair = lax.ppermute(pair, "lat", within)
    ready, outer, middle, sums = pl.pallas_call(
        inner_kernel,
        out_shape=[
            jax.ShapeDtypeStruct((devices * (rows - 4) // rows, members, width), jnp.float32),
            jax.ShapeDtypeStruct((4, members, lons), jnp.float32),
            jax.ShapeDtypeStruct((4, members, lons), jnp.float32),
            jax.ShapeDtypeStruct((patches, 8, width // patches), jnp.float32),
        ],
        in_specs=[vmem] * 2 + [hbm] * 4,
        out_specs=[vmem] * 4,
        scratch_shapes=[pltpu.VMEM((rows, members, lons), jnp.float32)] * 2
        + [
            pltpu.SMEM((1, patches), jnp.int32),
            pltpu.VMEM((patches, slots), jnp.int32),
            pltpu.VMEM((patches, slots), jnp.float32),
            pltpu.VMEM((patches, slots), jnp.float32),
            pltpu.SemaphoreType.DMA((4,)),
        ],
        name="inner",
        compiler_params=small,
        cost_estimate=pl.CostEstimate(flops=10**9, bytes_accessed=4 * 10**6, transcendentals=0),
    )(background_members, by_tile(stencil_weight_table), *map(in_hbm, observations))
    pieces = pl.pallas_call(
        stencil_kernel,
        out_shape=jax.ShapeDtypeStruct((devices, members, width), jnp.float32),
        in_specs=[vmem] * 6,
        out_specs=vmem,
        scratch_shapes=[
            pltpu.VMEM((2, 8, lons), jnp.float32),
            pltpu.VMEM((8, members, lons), jnp.float32),
            pltpu.VMEM((2, 4, members, lons), jnp.float32),
        ],
        name="stencil",
        compiler_params=small,
    )(ready, outer, middle, by_tile(stencil_weight_table), pair, cross)
    return pieces, sums


def body(background_members, stencil_weight_table, obs_index, obs_count, obs_value, obs_weight):
    member_slice, lat_rows, lon_cells = background_members.shape
    devices = lax.axis_size("mem")
    width = lat_rows * lon_cells // devices
    observations = (obs_count, obs_index[0], obs_value[0], obs_weight[0])
    outgoing, sums = forecast(background_members, stencil_weight_table, devices, observations)
    arrived = lax.all_to_all(outgoing, "mem", split_axis=0, concat_axis=0, tiled=True)
    analysed = analyse(arrived.reshape(devices * member_slice, width), sums)
    returned = lax.all_to_all(
        analysed.reshape(devices, member_slice, width), "mem", split_axis=0, concat_axis=0, tiled=True
    )
    pieces = lon_cells // width
    return pl.pallas_call(
        return_kernel,
        out_shape=jax.ShapeDtypeStruct(background_members.shape, jnp.float32),
        in_specs=[pl.BlockSpec(memory_space=pltpu.VMEM)],
        out_specs=pl.BlockSpec(memory_space=pltpu.HBM),
        scratch_shapes=[
            pltpu.VMEM(background_members.shape, jnp.float32),
            pltpu.SemaphoreType.DMA((lat_rows // 8 * pieces,)),
        ],
        name="home",
        compiler_params=pltpu.CompilerParams(vmem_limit_bytes=12 << 20),
    )(returned.reshape(lat_rows, pieces, member_slice, width))


def solution(mesh):
    placed = (
        P("mem", "lat", None),
        P(None, "lat", None),
        P("lat", "mem", None),
        P("lat", "mem"),
        P("lat", "mem", None),
        P("lat", "mem", None),
    )
    return jax.shard_map(
        body, mesh=mesh, in_specs=placed, out_specs=P("mem", "lat", None), check_vma=False
    )
```

```python
import functools

import jax
import jax.numpy as jnp
from jax import lax
from jax.experimental import pallas as pl
from jax.experimental.pallas import tpu as pltpu
from jax.sharding import PartitionSpec as P


NS_ITERS = 8
LANES = 128
NT = (((1,), (1,)), ((), ()))


def edge_kernel(x_hbm, w_hbm, pair_ref, cross_ref, x_ref, w_ref, sems):
    copies = [
        pltpu.make_async_copy(x_hbm, x_ref, sems.at[0]),
        pltpu.make_async_copy(w_hbm, w_ref, sems.at[1]),
    ]
    for copy in copies:
        copy.start()
    for copy in copies:
        copy.wait()
    members, rows, lons = x_ref.shape
    even = lax.rem(lax.axis_index("lat"), 2) == 0

    def pack(out_ref, near, far):
        for k in range(members):
            out_ref[k : k + 1, :lons] = x_ref[k, near : near + 1]
            out_ref[k : k + 1, lons : 2 * lons] = x_ref[k, far : far + 1]
        for run in range(5 * lons // LANES):
            t, start = run // (lons // LANES), run % (lons // LANES) * LANES
            place = 2 * lons + run // members * LANES
            out_ref[run % members : run % members + 1, place : place + LANES] = w_ref[
                t, near : near + 1, start : start + LANES
            ]

    @pl.when(even)
    def _():
        pack(pair_ref, rows - 1, rows - 2)
        pack(cross_ref, 0, 1)

    @pl.when(jnp.logical_not(even))
    def _():
        pack(pair_ref, 0, 1)
        pack(cross_ref, rows - 1, rows - 2)


def step(src_ref, r, wide):
    lons = src_ref.shape[2]
    centre = src_ref[r]
    return (
        wide(0) * centre
        + wide(1) * src_ref[r - 1]
        + wide(2) * src_ref[r + 1]
        + wide(3) * pltpu.roll(centre, lons - 1, 1)
        + wide(4) * pltpu.roll(centre, 1, 1)
    )


def weights_of(w_ref, r, rows, members, tiles):
    def wide(t):
        start = (t * rows // 8 + r // 8) * tiles * 8 + r % 8
        return jnp.concatenate(
            [w_ref[pl.ds(start + 8 * j, members, stride=0), :] for j in range(tiles)], axis=1
        )

    return wide


def inner_kernel(
    x_ref, w_ref, count_hbm, index_hbm, value_hbm, weight_hbm,
    ready_ref, outer_ref, near_ref, sums_ref,
    field_ref, middle_ref, count_ref, index_ref, value_ref, weight_ref, sems,
):
    copies = [
        pltpu.make_async_copy(source, target, sems.at[i])
        for i, (source, target) in enumerate(
            (
                (count_hbm, count_ref),
                (index_hbm, index_ref),
                (value_hbm, value_ref),
                (weight_hbm, weight_ref),
            )
        )
    ]
    for copy in copies:
        copy.start()
    rows, members, lons = field_ref.shape
    half = ready_ref.shape[2]
    own = lambda r: weights_of(w_ref, r, rows, members, lons // LANES)
    part = 2 * LANES
    for block in range(0, rows, 8):
        for start in range(0, lons, part):
            field_ref[block : block + 8, :, start : start + part] = jnp.swapaxes(
                x_ref[:, block : block + 8, start : start + part], 0, 1
            )
    for place, r in enumerate((0, 1, rows - 2, rows - 1)):
        outer_ref[place] = field_ref[r]

    def first(r, carry):
        middle_ref[r] = step(field_ref, r, own(r))
        return carry

    def second(r, carry):
        done = step(middle_ref, r, own(r))
        for h in range(lons // half):
            ready_ref[(r - 2) * (lons // half) + h] = done[:, h * half : (h + 1) * half]
        return carry

    lax.fori_loop(1, rows - 1, first, 0, unroll=2)
    for place, r in enumerate((1, 2, rows - 3, rows - 2)):
        near_ref[place] = middle_ref[r]
    lax.fori_loop(2, rows - 2, second, 0, unroll=2)
    for copy in copies:
        copy.wait()
    slot = lax.broadcasted_iota(jnp.int32, (1, index_ref.shape[1]), 1)
    for b in range(index_ref.shape[0]):
        weights = jnp.where(slot < count_ref[0, b], weight_ref[b : b + 1, :], 0.0)
        weight_sum, value_sum = cell_sums(
            index_ref[b : b + 1, :], weights, value_ref[b : b + 1, :], sums_ref.shape[2]
        )
        sums_ref[b, 0:1] = weight_sum
        sums_ref[b, 1:2] = value_sum


def stencil_kernel(ready_ref, outer_ref, middle_in, w_ref, pair_ref, cross_ref, out_ref, side_ref, rim_ref, near_ref):
    members, lons = outer_ref.shape[1:]
    count, _, half = out_ref.shape
    rows = count * half // lons
    rim = 2 * (lons // half)
    out_ref[rim : count - rim] = ready_ref[...]
    even = lax.rem(lax.axis_index("lat"), 2) == 0

    def unpack(ref, near, far, side):
        rim_ref[near] = ref[:, :lons]
        rim_ref[far] = ref[:, lons : 2 * lons]
        for run in range(5 * lons // LANES):
            t, start = run // (lons // LANES), run % (lons // LANES) * LANES
            place = 2 * lons + run // members * LANES
            side_ref[side, t : t + 1, start : start + LANES] = ref[
                run % members : run % members + 1, place : place + LANES
            ]

    @pl.when(even)
    def _():
        unpack(pair_ref, 6, 7, 1)
        unpack(cross_ref, 1, 0, 0)

    @pl.when(jnp.logical_not(even))
    def _():
        unpack(pair_ref, 1, 0, 0)
        unpack(cross_ref, 6, 7, 1)

    for place in range(4):
        rim_ref[place + 2] = outer_ref[place]
    for side in range(2):
        for place in range(2):
            near_ref[side, 2 - 2 * side + place] = middle_in[2 * side + place]
    own = lambda r: weights_of(w_ref, r, rows, members, lons // LANES)
    beyond = lambda side: lambda t: jnp.broadcast_to(side_ref[side, t : t + 1], (members, lons))
    near_ref[0, 0] = step(rim_ref, 1, beyond(0))
    near_ref[0, 1] = step(rim_ref, 2, own(0))
    near_ref[1, 2] = step(rim_ref, 5, own(rows - 1))
    near_ref[1, 3] = step(rim_ref, 6, beyond(1))

    def put(r, done):
        for h in range(lons // half):
            out_ref[r * (lons // half) + h] = done[:, h * half : (h + 1) * half]

    for side, place, r in ((0, 1, 0), (0, 2, 1), (1, 1, rows - 2), (1, 2, rows - 1)):
        put(r, step(near_ref.at[side], place, own(r)))


def return_kernel(in_ref, out_hbm, field_ref, sems):
    rows, pieces, _, width = in_ref.shape
    part = 4 * LANES
    copies = []
    for block in range(0, rows, 8):
        for h in range(pieces):
            for start in range(0, width, part):
                place = (slice(None), pl.ds(block, 8), pl.ds(h * width + start, part))
                field_ref[place] = jnp.swapaxes(
                    in_ref[block : block + 8, h, :, start : start + part], 0, 1
                )
                copies.append(
                    pltpu.make_async_copy(
                        field_ref.at[place], out_hbm.at[place], sems.at[len(copies)]
                    )
                )
                copies[-1].start()
    for copy in copies:
        copy.wait()


def by_tile(x):
    a, rows, lanes = x.shape
    x = x.reshape(a, rows // 8, 8, lanes // LANES, LANES)
    return jnp.swapaxes(x, 2, 3).reshape(-1, LANES)


def halves(x):
    lead = x.astype(jnp.bfloat16)
    return lead, (x - lead.astype(jnp.float32)).astype(jnp.bfloat16)


def cell_sums(indices, weights, values, cells):
    groups = cells // LANES
    group, lane = indices // LANES, indices % LANES
    row = lax.broadcasted_iota(jnp.int32, (2 * groups, indices.shape[1]), 0)
    both = jnp.where(row < groups, weights, weights * values)
    left = jnp.where(row % groups == group, both, 0.0)
    hit = lax.broadcasted_iota(jnp.int32, (LANES, indices.shape[1]), 0) == lane
    right = jnp.where(hit, 1.0, 0.0).astype(jnp.bfloat16)
    first = left.astype(jnp.bfloat16)
    rest = left - first.astype(jnp.float32)
    second = rest.astype(jnp.bfloat16)
    third = (rest - second.astype(jnp.float32)).astype(jnp.bfloat16)
    parts = jnp.concatenate([third, second, first], axis=0)
    dots = lax.dot_general(parts, right, NT, preferred_element_type=jnp.float32)
    height = 2 * groups
    total = (dots[:height] + dots[height : 2 * height]) + dots[2 * height :]
    rows = [
        jnp.concatenate([total[s + g : s + g + 1] for g in range(groups)], axis=1)
        for s in (0, groups)
    ]
    return rows


def analysis_kernel(sums_ref, x_ref, out_ref, *scratch):
    patches = sums_ref.shape[0]
    members = x_ref.shape[0]
    cells = x_ref.shape[1] // patches
    matrix_ref, root_ref, spread_ref, left_ref, right_ref = scratch[:5]
    totals = [scratch[5 + 3 * b : 8 + 3 * b] for b in range(patches)]
    identity = jnp.where(
        lax.broadcasted_iota(jnp.int32, (members, members), 0)
        == lax.broadcasted_iota(jnp.int32, (members, members), 1),
        1.0,
        0.0,
    )
    each = range(patches)
    chunks = [pl.ds(c, members) for c in range(0, cells, members)]
    LEAD, REST = 0, 1

    def load(b, lead, rest, transpose=False):
        if lead is not None:
            pltpu.matmul_push_rhs(lead, LEAD, b, transpose=transpose)
        if rest is not None:
            pltpu.matmul_push_rhs(rest, REST, b, transpose=transpose)

    stream = lambda total, rows, use=None: pltpu.matmul_acc_lhs(total, rows, load_staged_rhs=use)

    def set_root(b, root):
        root_ref[b] = root
        left_ref[b, LEAD, :, :members], left_ref[b, REST, :, :members] = halves(root)

    means, projections, scales = [], [], []
    for b in each:
        x = x_ref[:, b * cells : (b + 1) * cells]
        mean = jnp.sum(x, axis=0, keepdims=True) * (1.0 / members)
        spread = x - mean
        weight_sum, value_sum = sums_ref[b, 0:1], sums_ref[b, 1:2]
        spread_ref[b, LEAD], spread_ref[b, REST] = halves(spread)
        left_ref[b, LEAD], left_ref[b, REST] = halves(spread * weight_sum)
        misfit = value_sum - weight_sum * mean
        projections.append(jnp.sum(spread * misfit, axis=1, keepdims=True))
        means.append(mean)
    for chunk in chunks:
        for b in each:
            load(b, spread_ref[b, LEAD, :, chunk], spread_ref[b, REST, :, chunk], transpose=True)
            stream(totals[b][0], left_ref[b, LEAD, :, chunk], LEAD)
            stream(totals[b][0], left_ref[b, REST, :, chunk])
            stream(totals[b][0], left_ref[b, LEAD, :, chunk], REST)
    for b in each:
        gram = pltpu.matmul_pop(totals[b][0]) + (members - 1.0) * identity
        scale = jnp.sqrt(jnp.sum(gram * gram, keepdims=True))
        scales.append(scale)
        start = gram * (1.0 / scale)
        start = 0.5 * start
        matrix_ref[b] = start
        set_root(b, 1.5 * identity - start)
        right_ref[b, LEAD], right_ref[b, REST] = halves(start)

    def open_step(b):
        load(b, right_ref[b, LEAD], right_ref[b, REST])
        stream(totals[b][0], right_ref[b, LEAD], LEAD)
        load(b, right_ref[b, LEAD], None)
        stream(totals[b][0], right_ref[b, REST])
        stream(totals[b][0], right_ref[b, LEAD], REST)

    def close_step(b, with_root):
        if with_root:
            stream(totals[b][2], left_ref[b, LEAD, :, :members])
        factor = (2.25 * identity - 3.0 * matrix_ref[b]) + pltpu.matmul_pop(totals[b][0])
        lead, rest = halves(factor)
        stream(totals[b][1], lead)
        stream(totals[b][1], lead, LEAD)
        stream(totals[b][1], rest)
        if with_root:
            stream(totals[b][2], left_ref[b, LEAD, :, :members])
            stream(totals[b][2], left_ref[b, REST, :, :members])
        matrix = pltpu.matmul_pop(totals[b][1])
        matrix_ref[b] = matrix
        right_ref[b, LEAD], right_ref[b, REST] = halves(matrix)
        if with_root:
            set_root(b, 1.5 * root_ref[b] - pltpu.matmul_pop(totals[b][2]))

    for k in range(NS_ITERS - 1):
        for b in each:
            open_step(b)
        for b in each:
            close_step(b, k > 0)
    roots = []
    for b in each:
        load(b, right_ref[b, LEAD], right_ref[b, REST])
        lead, rest = left_ref[b, LEAD, :, :members], left_ref[b, REST, :, :members]
        stream(totals[b][0], lead, LEAD)
        stream(totals[b][0], rest)
        stream(totals[b][0], lead, REST)
    for b in each:
        root = 1.5 * root_ref[b] - pltpu.matmul_pop(totals[b][0])
        root_ref[b] = root
        roots.append(halves(root))
    for c, chunk in enumerate(chunks):
        for b in each:
            load(b, spread_ref[b, LEAD, :, chunk], spread_ref[b, REST, :, chunk])
            stream(totals[b][c], roots[b][0], LEAD)
            stream(totals[b][c], roots[b][1])
            stream(totals[b][c], roots[b][0], REST)
    for b in each:
        along = jnp.sum(root_ref[b] * projections[b], axis=0, keepdims=True)
        mover = jnp.sum(root_ref[b] * along, axis=1, keepdims=True) / scales[b]
        gain = jnp.sqrt((members - 1.0) / scales[b])
        for c, chunk in enumerate(chunks):
            place = slice(b * cells + c * members, b * cells + (c + 1) * members)
            mean = means[b][:, c * members : (c + 1) * members]
            spread = x_ref[:, place] - mean
            shift = mean + jnp.sum(spread * mover, axis=0, keepdims=True)
            out_ref[:, place] = shift + gain * pltpu.matmul_pop(totals[b][c])


def analyse(arrived, sums):
    members, width = arrived.shape
    patches = sums.shape[0]
    cells = width // patches
    vmem = pl.BlockSpec(memory_space=pltpu.VMEM)
    square = (members, members)
    kernel = lambda *refs: pl.run_scoped(
        functools.partial(analysis_kernel, *refs),
        *(pltpu.ACC(b)(square, jnp.float32) for b in range(patches) for _ in range(3)),
    )
    return pl.pallas_call(
        kernel,
        out_shape=jax.ShapeDtypeStruct(arrived.shape, jnp.float32),
        in_specs=[vmem] * 2,
        out_specs=vmem,
        scratch_shapes=[
            pltpu.VMEM((patches, *square), jnp.float32),
            pltpu.VMEM((patches, *square), jnp.float32),
            pltpu.VMEM((patches, 2, members, cells), jnp.bfloat16),
            pltpu.VMEM((patches, 2, members, cells), jnp.bfloat16),
            pltpu.VMEM((patches, 2, *square), jnp.bfloat16),
        ],
        name="analysis",
        compiler_params=pltpu.CompilerParams(vmem_limit_bytes=16 << 20),
    )(sums, arrived)


def forecast(background_members, stencil_weight_table, devices, observations):
    patches, slots = observations[1].shape
    in_hbm = lambda array: pltpu.with_memory_space_constraint(array, pltpu.HBM)
    members, rows, lons = background_members.shape
    width = rows * lons // devices
    vmem = pl.BlockSpec(memory_space=pltpu.VMEM)
    hbm = pl.BlockSpec(memory_space=pltpu.HBM)
    small = pltpu.CompilerParams(vmem_limit_bytes=12 << 20)
    packed = jax.ShapeDtypeStruct((members, 2 * lons + 5 * lons // members), jnp.float32)
    pair, cross = pl.pallas_call(
        edge_kernel,
        out_shape=[packed, packed],
        in_specs=[hbm] * 2,
        out_specs=[vmem] * 2,
        scratch_shapes=[
            pltpu.VMEM(background_members.shape, jnp.float32),
            pltpu.VMEM(stencil_weight_table.shape, jnp.float32),
            pltpu.SemaphoreType.DMA((2,)),
        ],
        name="edges",
        compiler_params=small,
    )(
        pltpu.with_memory_space_constraint(background_members, pltpu.HBM),
        pltpu.with_memory_space_constraint(stencil_weight_table, pltpu.HBM),
    )
    bands = lax.axis_size("lat")
    within = [(i, i ^ 1) for i in range(bands)]
    across = [(i, i - 1 + 2 * (i % 2)) for i in range(1, bands - 1)]
    cross = lax.ppermute(cross, "lat", across)
    pair = lax.ppermute(pair, "lat", within)
    ready, outer, middle, sums = pl.pallas_call(
        inner_kernel,
        out_shape=[
            jax.ShapeDtypeStruct((devices * (rows - 4) // rows, members, width), jnp.float32),
            jax.ShapeDtypeStruct((4, members, lons), jnp.float32),
            jax.ShapeDtypeStruct((4, members, lons), jnp.float32),
            jax.ShapeDtypeStruct((patches, 8, width // patches), jnp.float32),
        ],
        in_specs=[vmem] * 2 + [hbm] * 4,
        out_specs=[vmem] * 4,
        scratch_shapes=[pltpu.VMEM((rows, members, lons), jnp.float32)] * 2
        + [
            pltpu.SMEM((1, patches), jnp.int32),
            pltpu.VMEM((patches, slots), jnp.int32),
            pltpu.VMEM((patches, slots), jnp.float32),
            pltpu.VMEM((patches, slots), jnp.float32),
            pltpu.SemaphoreType.DMA((4,)),
        ],
        name="inner",
        compiler_params=small,
        cost_estimate=pl.CostEstimate(flops=10**9, bytes_accessed=4 * 10**6, transcendentals=0),
    )(background_members, by_tile(stencil_weight_table), *map(in_hbm, observations))
    pieces = pl.pallas_call(
        stencil_kernel,
        out_shape=jax.ShapeDtypeStruct((devices, members, width), jnp.float32),
        in_specs=[vmem] * 6,
        out_specs=vmem,
        scratch_shapes=[
            pltpu.VMEM((2, 8, lons), jnp.float32),
            pltpu.VMEM((8, members, lons), jnp.float32),
            pltpu.VMEM((2, 4, members, lons), jnp.float32),
        ],
        name="stencil",
        compiler_params=small,
    )(ready, outer, middle, by_tile(stencil_weight_table), pair, cross)
    return pieces, sums


def body(background_members, stencil_weight_table, obs_index, obs_count, obs_value, obs_weight):
    member_slice, lat_rows, lon_cells = background_members.shape
    devices = lax.axis_size("mem")
    width = lat_rows * lon_cells // devices
    observations = (obs_count, obs_index[0], obs_value[0], obs_weight[0])
    outgoing, sums = forecast(background_members, stencil_weight_table, devices, observations)
    arrived = lax.all_to_all(outgoing, "mem", split_axis=0, concat_axis=0, tiled=True)
    analysed = analyse(arrived.reshape(devices * member_slice, width), sums)
    returned = lax.all_to_all(
        analysed.reshape(devices, member_slice, width), "mem", split_axis=0, concat_axis=0, tiled=True
    )
    pieces = lon_cells // width
    return pl.pallas_call(
        return_kernel,
        out_shape=jax.ShapeDtypeStruct(background_members.shape, jnp.float32),
        in_specs=[pl.BlockSpec(memory_space=pltpu.VMEM)],
        out_specs=pl.BlockSpec(memory_space=pltpu.HBM),
        scratch_shapes=[
            pltpu.VMEM(background_members.shape, jnp.float32),
            pltpu.SemaphoreType.DMA((lat_rows // 8 * lon_cells // (4 * LANES),)),
        ],
        name="home",
        compiler_params=pltpu.CompilerParams(vmem_limit_bytes=12 << 20),
    )(returned.reshape(lat_rows, pieces, member_slice, width))


def solution(mesh):
    placed = (
        P("mem", "lat", None),
        P(None, "lat", None),
        P("lat", "mem", None),
        P("lat", "mem"),
        P("lat", "mem", None),
        P("lat", "mem", None),
    )
    return jax.shard_map(
        body, mesh=mesh, in_specs=placed, out_specs=P("mem", "lat", None), check_vma=False
    )
```
